512 devices in a mesh: vocab: 64 (over y, z), tp: 8 (over x, core).
Axes of the slice: x: 4, y: 4, z: 16, core: 2. Of those that a mesh axis runs over, the one named last changes fastest.
Arguments:
- residual: bfloat16 [512, 8192], P(None, 'tp'), may hold values from -64 to 64
- activation: bfloat16 [512, 16384], P('tp', 'vocab'), may hold values from -6 to 6
- down_weight: bfloat16 [16384, 8192], P('vocab', 'tp'), may hold values from -0.046875 to 0.046875
- norm_gain: float32 [8192], P('tp'), may hold values from 0.5 to 1.5
- head_weight: bfloat16 [8192, 81920], P('tp', 'vocab'), may hold values from -1 to 1
- allowed: int32 [512, 32], replicated, may hold values from 0 to 639, as said below
- tokens: int32 [512], P('tp'), may hold values from 0 to 81919, as said below
- lengths: int32 [4], replicated, may hold values from 1 to 128, as said below
- advantage_code: int32 [4], replicated, may hold values from -64 to 64
Outputs:
- policy_loss: float32 [], replicated
- down_gradient: bfloat16 [16384, 8192], P('vocab', 'tp')
- activation_gradient: bfloat16 [512, 16384], P('tp', 'vocab')
The draws below stay inside these ranges and needn't reach their ends.
Inputs may be any that keep to these rules, and one draw needn't show every extreme that they name: `allowed`: block numbers may repeat within a row; among the blocks v * 10 to (v + 1) * 10 - 1 of any one vocab index v, a row lists at most 4 different ones, and some row lists exactly 4. `tokens`: each row's token lies in a block that its row lists. `lengths`: at least one response has length 128.
All inputs are finite; a program needn't handle non-finite values.
Results may differ from the reference program's by a relative error of at most 0.0059.
Values may be sent and summed in bfloat16 or wider, within the bound.
A program may use at most 64 MiB of HBM per device.

```python
import math
import jax
import jax.numpy as jnp
from jax import lax

D = 8192
FF = 16384
BLK = 128
VBLK_DEV = 10
NBLK = 640
VOCAB = 81920
KB = 32
CAP = 4
SEQ = 128
RESP = 4
ROWS = 512
N_VOCAB = 64


def allowed_table(key):
    base_key = jax.random.fold_in(key, 11)
    keys = jax.random.split(base_key, 8)
    shard_first = jax.random.randint(keys[0], (ROWS,), 0, N_VOCAB)
    shard_second = jax.random.randint(keys[1], (ROWS,), 0, N_VOCAB)
    shard_order = jax.random.permutation(keys[2], N_VOCAB)
    start_shard = shard_order[shard_first * shard_second // N_VOCAB]
    inner_first = jax.random.randint(keys[3], (ROWS, KB), 0, VBLK_DEV)
    inner_second = jax.random.randint(keys[4], (ROWS, KB), 0, VBLK_DEV)
    inner_order = jax.random.permutation(keys[5], VBLK_DEV)
    inner_block = inner_order[inner_first * inner_second // VBLK_DEV]
    top_row = jax.random.randint(keys[6], (), 0, ROWS)
    low_row = (top_row + 1 + jax.random.randint(keys[7], (), 0, ROWS - 1)) % ROWS
    row_ids = jnp.arange(ROWS)
    start_shard = jnp.where(row_ids == top_row, N_VOCAB - 1, jnp.where(row_ids == low_row, 0, start_shard))
    slot_ids = jnp.arange(KB)
    group_ids = slot_ids // CAP
    within_ids = slot_ids % CAP
    first_group = (group_ids == 0)[None, :]
    inner_block = jnp.where((row_ids == top_row)[:, None] & first_group, VBLK_DEV - 1 - within_ids[None, :], inner_block)
    inner_block = jnp.where((row_ids == low_row)[:, None] & first_group, within_ids[None, :], inner_block)
    shard_ids = (start_shard[:, None] + group_ids[None, :]) % N_VOCAB
    table = shard_ids * VBLK_DEV + inner_block
    return (table.astype(jnp.int32), top_row, low_row)


def head_columns(key, column_ids):
    base_key = jax.random.fold_in(key, 37)
    raw_values = jax.vmap(lambda column: jax.random.normal(jax.random.fold_in(base_key, column), (D,), jnp.float32))(column_ids)
    values = jnp.clip(jnp.clip(raw_values, -4.5, 4.5) * (4.0 / math.sqrt(D)), -1.0, 1.0)
    feature_ids = jnp.arange(D)
    first_column = (column_ids == 0)[:, None]
    values = jnp.where(first_column & (feature_ids == 0)[None, :], 1.0, values)
    values = jnp.where(first_column & (feature_ids == 1)[None, :], -1.0, values)
    return values


def draw_head_weight(key, part):
    column_ids = jnp.arange(VOCAB, dtype=jnp.int32)
    return head_columns(key, column_ids).T.astype(jnp.bfloat16)


def draw_allowed(key, part):
    table, top_row, low_row = allowed_table(key)
    return table


def draw_tokens(key, part):
    table, top_row, low_row = allowed_table(key)
    base_key = jax.random.fold_in(key, 23)
    key_pick, key_inner = jax.random.split(base_key)
    pick_slot = jax.random.randint(key_pick, (ROWS,), 0, KB)
    chosen_block = jnp.sum(jnp.where(jnp.arange(KB)[None, :] == pick_slot[:, None], table, 0), axis=1)
    inner_index = jax.random.randint(key_inner, (ROWS,), 0, BLK)
    token_ids = chosen_block * BLK + inner_index
    row_ids = jnp.arange(ROWS)
    token_ids = jnp.where(row_ids == top_row, VOCAB - 1, token_ids)
    token_ids = jnp.where(row_ids == low_row, 0, token_ids)
    return token_ids.astype(jnp.int32)


def draw_lengths(key, part):
    base_key = jax.random.fold_in(key, 71)
    key_drawn, key_full = jax.random.split(base_key)
    drawn_values = jax.random.randint(key_drawn, (RESP,), 1, SEQ + 1)
    full_index = jax.random.randint(key_full, (), 0, RESP)
    return jnp.where(jnp.arange(RESP) == full_index, SEQ, drawn_values).astype(jnp.int32)


def draw_residual(key, part):
    base_key = jax.random.fold_in(key, 53)
    key_noise = jax.random.fold_in(base_key, 0)
    key_inner = jax.random.fold_in(base_key, 2)
    position = jnp.arange(D, dtype=jnp.float32) / (D - 1)
    values = jax.random.normal(key_noise, (ROWS, D), jnp.float32) * (1.0 + 2.0 * position)[None, :]
    table, top_row, low_row = allowed_table(key)
    row_ids = jnp.arange(ROWS)
    chosen_rows = row_ids % 16 == 5
    inner_index = jax.random.randint(key_inner, (ROWS,), 0, BLK - 1)
    first_column = table[:, 0] * BLK + inner_index
    first_vector = head_columns(key, first_column)
    second_vector = head_columns(key, first_column + 1)
    norm_first = jnp.sum(first_vector * first_vector, axis=1)
    norm_second = jnp.sum(second_vector * second_vector, axis=1)
    cross_term = jnp.sum(first_vector * second_vector, axis=1)
    base_strength = 40.0 * math.sqrt(D)
    strength = base_strength * jnp.where(row_ids % 3 == 0, 1.0, jnp.where(row_ids % 3 == 1, 2.0, 4.0))
    follow = strength * 0.99
    determinant = norm_first * norm_second - cross_term * cross_term
    coef_first = (norm_second * strength - cross_term * follow) / determinant
    coef_second = (norm_first * follow - cross_term * strength) / determinant
    aligned = coef_first[:, None] * first_vector + coef_second[:, None] * second_vector
    values = jnp.where(chosen_rows[:, None], aligned, values)
    values = jnp.clip(values, -64.0, 64.0)
    row_ids_all = jnp.arange(ROWS)[:, None]
    feature_ids = jnp.arange(D)[None, :]
    values = jnp.where((row_ids_all == 0) & (feature_ids == 0), 64.0, values)
    values = jnp.where((row_ids_all == 0) & (feature_ids == 1), -64.0, values)
    return values.astype(jnp.bfloat16)


def plant(values, key, least, largest):
    longest = values.shape.index(max(values.shape))
    spots = []
    for shift in (0, 1):
        where = [jax.random.randint(jax.random.fold_in(key, axis), (), 0, length) for axis, length in enumerate(values.shape)]
        where[longest] = (where[longest] + shift) % values.shape[longest]
        spots.append(tuple(where))
    return values.at[spots[0]].set(least).at[spots[1]].set(largest)


def steps_of(rng, dims, pieces, least, high):
    gain = 1.0
    for axis_at, shards_of in pieces:
        heights = jax.random.uniform(jax.random.fold_in(jax.random.fold_in(rng, 6), axis_at), (shards_of,), jnp.float32, least / len(pieces), high / len(pieces))
        gain = gain * jnp.repeat(jnp.exp(heights), dims[axis_at] // shards_of).reshape((-1,) + (1,) * (len(dims) - 1 - axis_at))
    return gain


def gaussian(own_key, extent, scale, bound, pieces=(), kind=jnp.bfloat16):
    values = jax.random.normal(own_key, extent, jnp.float32) * scale
    if len(pieces) > 0:
        values = steps_of(own_key, extent, pieces, -0.22, 0.18) * values
    return jnp.clip(values, min=-bound, max=bound).astype(kind)


def setup_inputs(seed: int = 0) -> dict:
    key_list = jax.random.split(jax.random.key(seed), 10)
    residual = draw_residual(jax.random.fold_in(key_list[9], 71), 0)
    activation = gaussian(key_list[1], (ROWS, FF), 1.0, 6.0, ((0, 8), (1, 64)))
    down_weight = gaussian(key_list[2], (FF, D), FF ** -0.5, 0.046875, ((0, 64), (1, 8)))
    norm_gain = jnp.clip(1.0 + 0.1 * jax.random.normal(key_list[3], (D,), jnp.float32), 0.5, 1.5)
    head_weight = draw_head_weight(jax.random.fold_in(key_list[9], 71), 0)
    allowed = draw_allowed(jax.random.fold_in(key_list[9], 71), 0)
    tokens = draw_tokens(jax.random.fold_in(key_list[9], 71), 0)
    lengths = draw_lengths(jax.random.fold_in(key_list[9], 71), 0)
    advantage_code = plant(jax.random.randint(key_list[8], (RESP,), -64, 65), jax.random.fold_in(key_list[8], 1), -64, 64).astype(jnp.int32)
    return dict(residual=residual, activation=activation, down_weight=down_weight, norm_gain=norm_gain, head_weight=head_weight, allowed=allowed, tokens=tokens, lengths=lengths, advantage_code=advantage_code)


def lookup_small(table, index_row):
    match = index_row[:, None] == jnp.arange(table.shape[0], dtype=jnp.int32)[None, :]
    return lax.optimization_barrier(jnp.sum(jnp.where(match, table[None, :], 0), axis=1))

def reference(residual, activation, down_weight, norm_gain, head_weight, allowed, tokens, lengths, advantage_code):
    mixed_term = jnp.dot(activation, down_weight, preferred_element_type=jnp.float32)
    hidden = residual.astype(jnp.float32) + mixed_term
    inv_rms = lax.rsqrt(lax.optimization_barrier(jnp.mean(hidden * hidden, axis=1, keepdims=True)) + 1e-06)
    normed = (hidden * inv_rms * norm_gain).astype(jnp.bfloat16)
    logits = jnp.dot(normed, head_weight, preferred_element_type=jnp.float32)
    block_ids = jnp.arange(NBLK, dtype=jnp.int32)
    block_ok = jnp.any(allowed[:, :, None] == block_ids[None, None, :], axis=1)
    permitted = jnp.repeat(block_ok, BLK, axis=1)
    row_peak = lax.optimization_barrier(jnp.max(jnp.where(permitted, logits, -1e+30), axis=1, keepdims=True))
    shifted = jnp.where(permitted, jnp.exp(logits - row_peak), 0.0)
    exp_total = lax.optimization_barrier(jnp.sum(shifted, axis=1, keepdims=True))
    column_ids = jnp.arange(VOCAB, dtype=jnp.int32)
    onehot = column_ids[None, :] == tokens[:, None]
    target = lax.optimization_barrier(jnp.sum(jnp.where(onehot, logits, 0.0), axis=1))
    log_prob = target - row_peak[:, 0] - jnp.log(exp_total[:, 0])
    row_ids = jnp.arange(ROWS, dtype=jnp.int32)
    response = row_ids // SEQ
    valid_row = row_ids % SEQ < lookup_small(lengths, response)
    advantage = lookup_small(advantage_code, response).astype(jnp.float32) / 32.0
    weight = jnp.where(valid_row, advantage, 0.0)
    policy_loss = -jnp.sum(weight * log_prob) / jnp.sum(lengths).astype(jnp.float32)
    probability = shifted / exp_total
    dlogits = (weight[:, None] * (probability - onehot.astype(jnp.float32))).astype(jnp.bfloat16)
    dnormed = lax.dot_general(dlogits, head_weight, (((1,), (1,)), ((), ())), preferred_element_type=jnp.float32)
    gained = dnormed * norm_gain
    gain_dot = lax.optimization_barrier(jnp.sum(gained * hidden, axis=1, keepdims=True))
    dhidden = (inv_rms * gained - hidden * (inv_rms * inv_rms * inv_rms) * gain_dot / D).astype(jnp.bfloat16)
    down_gradient = lax.dot_general(activation, dhidden, (((0,), (0,)), ((), ())), preferred_element_type=jnp.float32).astype(jnp.bfloat16)
    activation_gradient = lax.dot_general(dhidden, down_weight, (((1,), (1,)), ((), ())), preferred_element_type=jnp.float32).astype(jnp.bfloat16)
    return (policy_loss, down_gradient, activation_gradient)
```

```python
import jax
import jax.numpy as jnp
from jax import lax
from jax.experimental import pallas as pl
from jax.experimental.pallas import tpu as pltpu
from jax.sharding import PartitionSpec as P

MESH = pl.DeviceIdType.MESH
F32 = jnp.float32
BF16 = jnp.bfloat16
D = 8192
BLK = 128
CAP = 4
NB = 10
NY = 4
NZ = 16
NX = 4
NEG = -1e30
NC = 2
CW = 1024 // NC
DW = CAP * BLK + BLK
N_SEND = 200
NT = (((1,), (1,)), ((), ()))


def kernel(
    res_hbm,
    act_hbm,
    w_hbm,
    gain_ref,
    head_hbm,
    allowed_ref,
    tok_ref,
    len_ref,
    adv_ref,
    loss_ref,
    dg_ref,
    ag_ref,
    res,
    act,
    actt,
    w,
    head,
    slotb,
    own,
    s1,
    ry1,
    t1,
    s1a,
    ra1,
    t1a,
    s1b,
    rb1,
    hid,
    ssq,
    nrm,
    s2,
    ry2,
    s2a,
    ra2,
    s2b,
    rb2,
    dhg,
    lhs,
    lb,
    lp,
    lpr,
    lx,
    lxr,
    lg,
    stz,
    sty,
    dl,
    gs,
    lhs2,
    dh,
    ags,
    agr,
    los,
    lsem,
    ssem,
    rsem,
):
    v = lax.axis_index("vocab")
    t = lax.axis_index("tp")
    y = v // NZ
    z = v % NZ
    x = t // 2
    c = t % 2
    k0 = z % 4
    m0 = z // 4

    def dev_y(d):
        return (((y + d) % NY) * NZ + z, t)

    def dev_z(d):
        return (y * NZ + (z + d) % NZ, t)

    def dev_t(d):
        return (v, (t + d) % 8)

    def dev_x(d):
        return (v, ((x + d) % NX) * 2 + c)

    partner = (v, x * 2 + (1 - c))

    barrier = pltpu.get_barrier_semaphore()
    peers = (
        [dev_t(d) for d in range(1, 8)]
        + [dev_y(d) for d in range(1, 4)]
        + [dev_z(d) for d in (1, 2, 4, 8, 12, 14, 15)]
    )
    for dev in peers:
        pl.semaphore_signal(barrier, inc=1, device_id=dev, device_id_type=MESH)

    loads = [
        pltpu.make_async_copy(act_hbm, act.at[t], lsem.at[0]),
        pltpu.make_async_copy(w_hbm, w, lsem.at[1]),
        pltpu.make_async_copy(res_hbm.at[y * 16 + k0 * 4 + m0], res, lsem.at[2]),
        pltpu.make_async_copy(head_hbm, head, lsem.at[3]),
    ]
    for copy in loads:
        copy.start()

    first_block = v * NB

    def prep(i, carry):
        rows = pl.ds(pl.multiple_of(i * 128, 128), 128)
        listed = allowed_ref[rows, :]
        run = jnp.zeros((128, 1), F32)
        for b in range(NB):
            hit = jnp.max(
                jnp.where(listed == first_block + b, 1.0, 0.0).astype(F32), axis=1, keepdims=True
            )
            slot = jnp.where(hit > 0.5, run, 99.0)
            run = run + hit
            slotb[b, rows, :] = jnp.broadcast_to(slot, (128, 128))
        return carry

    lax.fori_loop(0, 4, prep, 0)

    sends = []
    count = [0]

    def rcopy(src, dst, dev):
        i = count[0]
        count[0] += 1
        copy = pltpu.make_async_remote_copy(
            src_ref=src,
            dst_ref=dst,
            send_sem=ssem.at[i],
            recv_sem=rsem.at[i],
            device_id=dev,
            device_id_type=MESH,
        )
        copy.start()
        sends.append(copy)
        return copy

    loads[0].wait()
    pl.semaphore_wait(barrier, len(peers))

    a_in = {}
    for d in (4, 3, 5, 2, 6, 1, 7):
        a_in[d] = rcopy(act.at[t], act.at[t], dev_t(d))
    loads[1].wait()
    for d in range(1, 8):
        a_in[d].wait_recv()

    def act_rows(yb):
        return jnp.concatenate([act[2 * yb], act[2 * yb + 1]], axis=0)

    def rs_y(s, ry, d, yb):
        return [
            rcopy(
                s.at[pl.ds(n * 64 + yb * 16, 16)],
                ry.at[pl.ds(((d - 1) * NC + n) * 16, 16)],
                dev_y(d),
            )
            for n in range(NC)
        ]

    def rs_rest(y_in, ry, sa, ra, sb, rb, use):
        a_in, b_in = [], []
        for n in range(NC):
            total = own[n * 16 : (n + 1) * 16]
            for d in (1, 3, 2):
                y_in[d][n].wait_recv()
            for d in (1, 3, 2):
                q = (d - 1) * NC + n
                total = total + ry[q * 16 : (q + 1) * 16].astype(F32)
            t1[n * 16 : (n + 1) * 16] = total
            sa[n * 16 : (n + 1) * 16] = total.astype(BF16)
            far = 2 if n % 2 == 0 else 14
            a_in.append(
                [
                    rcopy(
                        sa.at[pl.ds(n * 16 + ((k0 + dz) % 4) * 4, 4)],
                        ra.at[pl.ds((j * NC + n) * 4, 4)],
                        dev_z(dz),
                    )
                    for j, dz in ((2, far), (0, 1), (1, 15))
                ]
            )
        for n in range(NC):
            for copy in a_in[n]:
                copy.wait_recv()
            total = t1[pl.ds(n * 16 + k0 * 4, 4)]
            for j in range(3):
                q = j * NC + n
                total = total + ra[q * 4 : (q + 1) * 4].astype(F32)
            t1a[n * 4 : (n + 1) * 4] = total
            sb[n * 4 : (n + 1) * 4] = total.astype(BF16)
            b_in.append(
                [
                    rcopy(
                        sb.at[pl.ds(n * 4 + (m0 + dm) % 4, 1)],
                        rb.at[pl.ds((dm - 1) * NC + n, 1)],
                        dev_z(4 * dm),
                    )
                    for dm in (2, 1, 3)
                ]
            )
        for n in range(NC):
            for copy in b_in[n]:
                copy.wait_recv()
            total = t1a[n * 4 + m0]
            for dm in range(3):
                total = total + rb[dm * NC + n].astype(F32)
            use(n, total)

    def gather(g):
        base = y * 16
        b_in, y_in = [], []

        def to_y(n, cls):
            rows = pl.ds(n * 64 + base + cls * 4, 4)
            return {d: rcopy(g.at[rows], g.at[rows], dev_y(d)) for d in (2, 1, 3)}

        for n in range(NC):
            row = pl.ds(n * 64 + base + k0 * 4 + m0, 1)
            b_in.append([rcopy(g.at[row], g.at[row], dev_z(4 * dm)) for dm in (2, 1, 3)])
        a_in = []
        for n in range(NC):
            for copy in b_in[n]:
                copy.wait_recv()
            rows = pl.ds(n * 64 + base + k0 * 4, 4)
            far = 2 if n % 2 == 0 else 14
            a_in.append([rcopy(g.at[rows], g.at[rows], dev_z(dz)) for dz in (far, 1, 15)])
            y_in.append([to_y(n, k0)])
        for n in range(NC):
            for j, dk in ((1, 3), (2, 1), (0, 2)):
                a_in[n][j].wait_recv()
                y_in[n].append(to_y(n, (k0 + dk) % 4))
        return y_in

    def gathered(g, y_in, d):
        if d > 0:
            for n in range(NC):
                for part in y_in[n]:
                    part[d].wait_recv()
        yb = (y + 4 - d) % 4
        pieces = [
            g[pl.ds(n * 64 + yb * 16, 16)].astype(F32).reshape(128, CW).astype(BF16)
            for n in range(NC)
        ]
        return yb, jnp.concatenate(pieces, axis=1)

    y_in = {}
    for d in (2, 1, 3, 0):
        yb = (y + d) % 4
        for n in range(NC):
            part = jnp.dot(act_rows(yb), w[:, n * CW : (n + 1) * CW], preferred_element_type=F32)
            part = part.reshape(16, 8, CW)
            if d == 0:
                own[n * 16 : (n + 1) * 16] = part
            else:
                s1[pl.ds(n * 64 + yb * 16, 16)] = part.astype(BF16)
        if d > 0:
            y_in[d] = rs_y(s1, ry1, d, yb)

    for i in range(8):
        actt[:, i * 64 : (i + 1) * 64] = act[i].astype(F32).T.astype(BF16)
    loads[2].wait()

    def use_hidden(n, total):
        hid[:, n * CW : (n + 1) * CW] = res[:, n * CW : (n + 1) * CW].astype(F32) + total

    rs_rest(y_in, ry1, s1a, ra1, s1b, rb1, use_hidden)

    h = hid[...]
    ssq[t] = jnp.broadcast_to(jnp.sum(h * h, axis=1, keepdims=True), (8, 128))
    ss_in = [rcopy(ssq.at[t], ssq.at[t], dev_t(d)) for d in (4, 3, 5, 2, 6, 1, 7)]
    for copy in ss_in:
        copy.wait_recv()
    square = ssq[0]
    for i in range(1, 8):
        square = square + ssq[i]
    inv_rms = lax.rsqrt(square[:, :1] / D + 1e-06)
    mine = y * 16 + k0 * 4 + m0
    for n in range(NC):
        cols = slice(n * CW, (n + 1) * CW)
        nrm[n * 64 + mine] = (hid[:, cols] * inv_rms * gain_ref[:, cols]).astype(BF16)
    y_in = gather(nrm)
    loads[3].wait()

    x_in = {}
    order = (0, 1, 3, 2)
    p_in = []
    for d in order:
        yb, block = gathered(nrm, y_in, d)
        lhs[...] = block

        def columns(j, carry):
            cols = pl.ds(pl.multiple_of(j * 256, 256), 256)
            lb[:, cols] = jnp.dot(lhs[...], head[:, cols], preferred_element_type=F32)
            return carry

        lax.fori_loop(0, 5, columns, 0)

        def compact(half, dst):
            rows = pl.ds(pl.multiple_of(half * 64, 64), 64)
            mask_rows = pl.ds(pl.multiple_of(yb * 128 + half * 64, 64), 64)
            out = [jnp.zeros((64, 128), F32) for _ in range(CAP)]
            for b in range(NB):
                slot = slotb[b, mask_rows, :]
                val = lb[rows, b * BLK : (b + 1) * BLK]
                for s in range(CAP):
                    out[s] = jnp.where(slot == float(s), val, out[s])
            for s in range(CAP):
                dst[:, s * BLK : (s + 1) * BLK] = out[s]

        compact(1 - c, lp.at[yb])
        p_in.append(rcopy(lp.at[yb], lpr.at[yb], partner))
        compact(c, lx.at[yb])
        if d != order[0]:
            combine(p_prev, yb_prev)
        p_prev, yb_prev = p_in[-1], yb

        def combine(copy, row_block):
            copy.wait_recv()
            lx[row_block] = lx[row_block] + lpr[row_block]

    combine(p_prev, yb_prev)
    x_in = {d: rcopy(lx.at[(x + d) % 4], lxr.at[d - 1], dev_x(d)) for d in (2, 1, 3)}
    total = lx[x]
    for d in (1, 3, 2):
        x_in[d].wait_recv()
        total = total + lxr[d - 1]
    lg[...] = total

    own_rows = pl.ds(pl.multiple_of(t * 64, 64), 64)
    lane = lax.broadcasted_iota(jnp.int32, (64, 128), 1)
    eye = lane == lax.broadcasted_iota(jnp.int32, (64, 128), 0)

    def to_row(col):
        return jnp.sum(jnp.where(eye, col, 0.0), axis=0, keepdims=True)

    def to_col(row):
        return jnp.sum(jnp.where(eye, row, 0.0), axis=1, keepdims=True)

    tok = to_col(tok_ref[...].astype(F32)).astype(jnp.int32)
    tok_block = (tok >> 7) - first_block
    tok_lane = tok & 127
    seen = jnp.zeros((64, 128), F32)
    tok_slot = jnp.full((64, 128), 99.0, F32)
    for b in range(NB):
        slot = slotb[b, own_rows, :]
        seen = seen + jnp.where(slot < 50.0, 1.0, 0.0)
        tok_slot = jnp.where(tok_block == b, slot, tok_slot)

    peak = jnp.full((64, 128), NEG, F32)
    for s in range(CAP):
        peak = jnp.maximum(peak, jnp.where(seen > float(s), lg[:, s * BLK : (s + 1) * BLK], NEG))
    peak = jnp.max(peak, axis=1, keepdims=True)
    zero = jnp.zeros((64, 128), F32)
    tot, mom, tgt = zero, zero, zero
    for s in range(CAP):
        val = lg[:, s * BLK : (s + 1) * BLK]
        ok = seen > float(s)
        shifted = jnp.where(ok, val - peak, 0.0)
        e = jnp.where(ok, jnp.exp(shifted), 0.0)
        tot = tot + e
        mom = mom + e * shifted
        tgt = tgt + jnp.where((tok_slot == float(s)) & (lane == tok_lane), val, 0.0)
    tot = jnp.sum(tot, axis=1, keepdims=True)
    mom = jnp.sum(mom, axis=1, keepdims=True)
    tgt = jnp.sum(tgt, axis=1, keepdims=True)
    at = k0 * 4 + m0
    stz[at] = jnp.concatenate(
        [to_row(peak), to_row(tot), to_row(mom), to_row(tgt), jnp.zeros((4, 128), F32)], axis=0
    )
    b_in = [rcopy(stz.at[at], stz.at[at], dev_z(4 * dm)) for dm in (2, 1, 3)]
    for copy in b_in:
        copy.wait_recv()
    rows = pl.ds(k0 * 4, 4)
    a_in = [rcopy(stz.at[rows], stz.at[rows], dev_z(dz)) for dz in (2, 1, 15)]
    for copy in a_in:
        copy.wait_recv()

    def join(parts):
        top = parts[0][0:1]
        for p in parts[1:]:
            top = jnp.maximum(top, p[0:1])
        tot = jnp.zeros((1, 128), F32)
        mom = jnp.zeros((1, 128), F32)
        tgt = jnp.zeros((1, 128), F32)
        for p in parts:
            gap = p[0:1] - top
            scale = jnp.exp(gap)
            tot = tot + p[1:2] * scale
            mom = mom + scale * (p[2:3] + p[1:2] * gap)
            tgt = tgt + p[3:4]
        return top, tot, mom, tgt

    top, tot, mom, tgt = join([stz[i] for i in range(NZ)])
    sty[y] = jnp.concatenate([top, tot, mom, tgt, jnp.zeros((4, 128), F32)], axis=0)
    y_st = [rcopy(sty.at[y], sty.at[y], dev_y(d)) for d in (2, 1, 3)]
    for copy in y_st:
        copy.wait_recv()
    top, tot, mom, tgt = join([sty[i] for i in range(NY)])
    top, tot, mom, tgt = to_col(top), to_col(tot), to_col(mom), to_col(tgt)

    response = t // 2
    length = jnp.int32(0)
    code = jnp.int32(0)
    length_sum = jnp.int32(0)
    for i in range(4):
        length = jnp.where(response == i, len_ref[i], length)
        code = jnp.where(response == i, adv_ref[i], code)
        length_sum = length_sum + len_ref[i]
    position = c * 64 + lax.broadcasted_iota(jnp.int32, (64, 1), 0)
    weight = jnp.where(position < length, code.astype(F32) / 32.0, 0.0)
    log_prob = tgt - top - jnp.log(tot)
    part = jnp.sum(weight * log_prob, axis=0, keepdims=True)
    gdot = weight * (mom / tot - (tgt - top))
    for s in range(CAP):
        val = lg[:, s * BLK : (s + 1) * BLK]
        prob = jnp.where(seen > float(s), jnp.exp(val - top), 0.0) / tot
        hot = jnp.where((tok_slot == float(s)) & (lane == tok_lane), 1.0, 0.0)
        dl[t, :, s * BLK : (s + 1) * BLK] = (weight * (prob - hot)).astype(BF16)
    g_hi = gdot.astype(BF16).astype(F32)
    g_mid = (gdot - g_hi).astype(BF16).astype(F32)
    g_lo = gdot - g_hi - g_mid
    tail = jnp.where(lane == 0, g_hi, jnp.where(lane == 1, g_mid, jnp.where(lane == 2, g_lo, 0.0)))
    dl[t, :, CAP * BLK :] = tail.astype(BF16)

    dx_in = {d: rcopy(dl.at[t], dl.at[t], dev_x(d)) for d in (2, 1, 3)}
    d_in = {0: rcopy(dl.at[t], dl.at[t], partner)}
    for d in (1, 3, 2):
        dx_in[d].wait_recv()
        slot = ((x + 4 - d) % 4) * 2 + c
        d_in[d] = rcopy(dl.at[slot], dl.at[slot], partner)
    los[t] = jnp.broadcast_to(part, (8, 128))
    loss_in = [rcopy(los.at[t], los.at[t], dev_t(d)) for d in range(1, 8)]
    for d in range(4):
        d_in[d].wait_recv()

    y_in = {}
    for d in (2, 1, 3, 0):
        yb = (y + d) % 4
        for half in range(2):
            rows = slice(half * 64, (half + 1) * 64)
            mask_rows = pl.ds(pl.multiple_of(yb * 128 + half * 64, 64), 64)
            vals = [
                dl[yb * 2 + half, :, s * BLK : (s + 1) * BLK].astype(F32) for s in range(CAP)
            ]
            for b in range(NB):
                slot = slotb[b, mask_rows, :]
                out = jnp.zeros((64, 128), F32)
                for s in range(CAP):
                    out = jnp.where(slot == float(s), vals[s], out)
                lhs2[rows, b * BLK : (b + 1) * BLK] = out.astype(BF16)
        for n in range(NC):
            for q in range(CW // 256):
                part_d = lax.dot_general(
                    lhs2[...],
                    head[n * CW + q * 256 : n * CW + (q + 1) * 256, :],
                    NT,
                    preferred_element_type=F32,
                ).reshape(16, 8, 256)
                cols = slice(q * 256, (q + 1) * 256)
                if d == 0:
                    own[n * 16 : (n + 1) * 16, :, cols] = part_d
                else:
                    s2[pl.ds(n * 64 + yb * 16, 16), :, cols] = part_d.astype(BF16)
        if d > 0:
            y_in[d] = rs_y(s2, ry2, d, yb)

    gs[...] = dl[y * 2 + k0 // 2, :, CAP * BLK :].astype(F32)
    gcol = jnp.sum(
        gs[pl.ds(pl.multiple_of(((k0 % 2) * 4 + m0) * 8, 8), 8), :], axis=1, keepdims=True
    )

    def use_dnormed(n, total):
        cols = slice(n * CW, (n + 1) * CW)
        value = inv_rms * (gain_ref[:, cols] * total) - hid[:, cols] * (
            inv_rms * inv_rms * gcol / D
        )
        dhg[n * 64 + mine] = value.astype(BF16)

    rs_rest(y_in, ry2, s2a, ra2, s2b, rb2, use_dnormed)
    y_in = gather(dhg)

    ag_in = {}
    for d in order:
        yb, block = gathered(dhg, y_in, d)
        dh[pl.ds(pl.multiple_of(yb * 128, 128), 128), :] = block
        part_a = lax.dot_general(block, w[...], NT, preferred_element_type=F32)
        ags[2 * yb] = part_a[:64]
        ags[2 * yb + 1] = part_a[64:]
    agb = agr.at[pl.ds(0, 8)]
    for i in range(8):
        agb[i] = ags[i].astype(BF16)
    for d in (4, 3, 5, 2, 6, 1, 7):
        ag_in[d] = rcopy(agr.at[(t + d) % 8], agr.at[8 + d], dev_t(d))
    dg_ref[...] = jnp.dot(actt[...], dh[...], preferred_element_type=F32).astype(BF16)
    for copy in loss_in:
        copy.wait_recv()
    objective = los[0]
    for i in range(1, 8):
        objective = objective + los[i]
    loss_ref[...] = -objective / length_sum.astype(F32)
    total = ags[t]
    for d in range(1, 8):
        ag_in[d].wait_recv()
        total = total + agr[8 + d].astype(F32)
    ag_ref[...] = total.astype(BF16)
    for copy in sends:
        copy.wait_send()


def body(
    residual,
    activation,
    down_weight,
    norm_gain,
    head_weight,
    allowed,
    tokens,
    lengths,
    advantage_code,
):
    any_spec = pl.BlockSpec(memory_space=pl.ANY)
    vmem = pl.BlockSpec(memory_space=pltpu.VMEM)
    smem = pl.BlockSpec(memory_space=pltpu.SMEM)
    v = pltpu.VMEM
    loss, dg, ag = pl.pallas_call(
        kernel,
        out_shape=(
            jax.ShapeDtypeStruct((8, 128), F32),
            jax.ShapeDtypeStruct((256, 1024), BF16),
            jax.ShapeDtypeStruct((64, 256), BF16),
        ),
        in_specs=[any_spec, any_spec, any_spec, vmem, any_spec, vmem, vmem, smem, smem],
        out_specs=(vmem, vmem, vmem),
        scratch_shapes=[
            v((8, 1024), BF16),
            v((8, 64, 256), BF16),
            v((256, 512), BF16),
            v((256, 1024), BF16),
            v((1024, 1280), BF16),
            v((NB, 512, 128), F32),
            v((NC * 16, 8, CW), F32),
            v((NC * 64, 8, CW), BF16),
            v((3 * NC * 16, 8, CW), BF16),
            v((NC * 16, 8, CW), F32),
            v((NC * 16, 8, CW), BF16),
            v((3 * NC * 4, 8, CW), BF16),
            v((NC * 4, 8, CW), F32),
            v((NC * 4, 8, CW), BF16),
            v((3 * NC, 8, CW), BF16),
            v((8, 1024), F32),
            v((8, 8, 128), F32),
            v((NC * 64, 8, CW), BF16),
            v((NC * 64, 8, CW), BF16),
            v((3 * NC * 16, 8, CW), BF16),
            v((NC * 16, 8, CW), BF16),
            v((3 * NC * 4, 8, CW), BF16),
            v((NC * 4, 8, CW), BF16),
            v((3 * NC, 8, CW), BF16),
            v((NC * 64, 8, CW), BF16),
            v((128, 1024), BF16),
            v((128, 1280), F32),
            v((4, 64, CAP * BLK), F32),
            v((4, 64, CAP * BLK), F32),
            v((4, 64, CAP * BLK), F32),
            v((3, 64, CAP * BLK), F32),
            v((64, CAP * BLK), F32),
            v((NZ, 8, 128), F32),
            v((NY, 8, 128), F32),
            v((8, 64, DW), BF16),
            v((64, 128), F32),
            v((128, 1280), BF16),
            v((512, 1024), BF16),
            v((8, 64, 256), F32),
            v((16, 64, 256), BF16),
            v((8, 8, 128), F32),
            pltpu.SemaphoreType.DMA((4,)),
            pltpu.SemaphoreType.DMA((N_SEND,)),
            pltpu.SemaphoreType.DMA((N_SEND,)),
        ],
        compiler_params=pltpu.CompilerParams(
            collective_id=0, has_side_effects=True, vmem_limit_bytes=60 * 1024 * 1024
        ),
        name="step",
    )(
        residual.reshape(64, 8, 1024),
        activation,
        down_weight,
        norm_gain.reshape(1, 1024),
        head_weight,
        allowed,
        jnp.pad(tokens.reshape(1, 64), ((0, 0), (0, 64))),
        lengths,
        advantage_code,
    )
    return loss[0, 0], dg, ag


def solution(mesh):
    in_specs = (
        P(None, "tp"),
        P("tp", "vocab"),
        P("vocab", "tp"),
        P("tp"),
        P("tp", "vocab"),
        P(),
        P("tp"),
        P(),
        P(),
    )
    out_specs = (P(), P("vocab", "tp"), P("tp", "vocab"))
    return jax.shard_map(body, mesh=mesh, in_specs=in_specs, out_specs=out_specs, check_vma=False)
```

```python
import jax
import jax.numpy as jnp
from jax import lax
from jax.experimental import pallas as pl
from jax.experimental.pallas import tpu as pltpu
from jax.sharding import PartitionSpec as P

MESH = pl.DeviceIdType.MESH
F32 = jnp.float32
BF16 = jnp.bfloat16
D = 8192
BLK = 128
CAP = 4
NB = 10
NY = 4
NZ = 16
NX = 4
NEG = -1e30
NC = 2
CW = 1024 // NC
N_SEND = 240
NT = (((1,), (1,)), ((), ()))


def kernel(
    res_hbm,
    act_hbm,
    w_hbm,
    gain_ref,
    head_hbm,
    allowed_ref,
    tok_ref,
    len_ref,
    adv_ref,
    actt,
    dh,
    ag_ref,
    loss_ref,
    res,
    act,
    w,
    head,
    slotb,
    own,
    fo,
    s1,
    f1,
    rp1,
    rm1,
    t1,
    s1a,
    ra1,
    t1a,
    s1b,
    rb1,
    hid,
    ssq,
    iv,
    ivy,
    nrm,
    s2,
    f2,
    rp2,
    rm2,
    s2a,
    ra2,
    s2b,
    rb2,
    dhg,
    lhs,
    lb,
    lp,
    lpr,
    lx,
    lxr,
    lg,
    stz,
    sty,
    dl,
    gv,
    lhs2,
    ags,
    agr,
    los,
    lsem,
    ssem,
    rsem,
):
    v = lax.axis_index("vocab")
    t = lax.axis_index("tp")
    y = v // NZ
    z = v % NZ
    x = t // 2
    c = t % 2
    k0 = z % 4
    m0 = z // 4

    def dev_y(d):
        return (((y + d) % NY) * NZ + z, t)

    def dev_z(d):
        return (y * NZ + (z + d) % NZ, t)

    def dev_t(d):
        return (v, (t + d) % 8)

    def dev_x(d):
        return (v, ((x + d) % NX) * 2 + c)

    partner = (v, x * 2 + (1 - c))

    barrier = pltpu.get_barrier_semaphore()
    peers = (
        [dev_t(d) for d in range(1, 8)]
        + [dev_y(d) for d in range(1, 4)]
        + [dev_z(d) for d in range(1, NZ)]
    )
    for dev in peers:
        pl.semaphore_signal(barrier, inc=1, device_id=dev, device_id_type=MESH)

    loads = [
        pltpu.make_async_copy(act_hbm, act.at[t], lsem.at[0]),
        pltpu.make_async_copy(w_hbm, w, lsem.at[1]),
        pltpu.make_async_copy(res_hbm.at[y * 16 + k0 * 4 + m0], res, lsem.at[2]),
        pltpu.make_async_copy(head_hbm, head, lsem.at[3]),
    ]
    for copy in loads:
        copy.start()

    first_block = v * NB

    def prep(i, carry):
        rows = pl.ds(pl.multiple_of(i * 128, 128), 128)
        listed = allowed_ref[:, rows]
        run = jnp.zeros((1, 128), F32)
        slots = []
        for b in range(NB):
            hit = jnp.max(
                jnp.where(listed == first_block + b, 1.0, 0.0).astype(F32), axis=0, keepdims=True
            )
            slots.append(jnp.where(hit > 0.5, run, 99.0))
            run = run + hit
        turned = jnp.concatenate(slots + [jnp.zeros((128 - NB, 128), F32)], axis=0).T
        for b in range(NB):
            slotb[b, rows, :] = jnp.broadcast_to(turned[:, b : b + 1], (128, 128))
        return carry

    lax.fori_loop(0, 4, prep, 0)

    sends = []
    count = [0]

    def rcopy(src, dst, dev):
        i = count[0]
        count[0] += 1
        copy = pltpu.make_async_remote_copy(
            src_ref=src,
            dst_ref=dst,
            send_sem=ssem.at[i],
            recv_sem=rsem.at[i],
            device_id=dev,
            device_id_type=MESH,
        )
        copy.start()
        sends.append(copy)
        return copy

    def reserve(k):
        i = count[0]
        count[0] += k
        return i

    def described(src, dst, dev, i):
        return pltpu.make_async_remote_copy(
            src_ref=src,
            dst_ref=dst,
            send_sem=ssem.at[i],
            recv_sem=rsem.at[i],
            device_id=dev,
            device_id_type=MESH,
        )

    loads[0].wait()
    pl.semaphore_wait(barrier, len(peers))

    a_in = [rcopy(act.at[t], act.at[t], dev_t(d)) for d in (4, 3, 5, 2, 6, 1, 7)]
    loads[1].wait()
    for copy in a_in:
        copy.wait_recv()

    def act_rows(yb):
        return jnp.concatenate([act[2 * yb], act[2 * yb + 1]], axis=0)

    def part16(n, k=16):
        return slice(n * k, (n + 1) * k)

    def rs_start(block, s, f, rp, rm):
        step_one, step_two = {}, {}
        far = (y + 2) % 4
        block(far, lambda n, cols, part: s.__setitem__(
            (pl.ds(n * 64 + far * 16, 16), slice(None), cols), part.astype(BF16)))
        for n in range(NC):
            step_one[n] = rcopy(
                s.at[pl.ds(n * 64 + far * 16, 16)], f.at[pl.ds(n * 16, 16)], dev_y(1 if n % 2 == 0 else 3)
            )
        for d, dst in ((1, rp), (3, rm)):
            yb = (y + d) % 4

            def put(n, cols, part, d=d, yb=yb):
                if (n % 2 == 0) == (d == 1):
                    fo[part16(n), :, cols] = part
                else:
                    s[pl.ds(n * 64 + yb * 16, 16), :, cols] = part.astype(BF16)

            block(yb, put)
            for n in range(NC):
                if (n % 2 == 0) != (d == 1):
                    rows = pl.ds(n * 64 + yb * 16, 16)
                    step_two[d, n] = rcopy(s.at[rows], dst.at[pl.ds(n * 16, 16)], dev_y(d))
        for n in range(NC):
            d, dst = ((1, rp), (3, rm))[n % 2]
            rows = pl.ds(n * 64 + ((y + d) % 4) * 16, 16)
            step_one[n].wait_recv()
            s[rows] = (fo[part16(n)] + f[part16(n)].astype(F32)).astype(BF16)
            step_two[d, n] = rcopy(s.at[rows], dst.at[pl.ds(n * 16, 16)], dev_y(d))

        def put_own(n, cols, part):
            own[part16(n), :, cols] = part

        block(y, put_own)
        return step_two

    def rs_rest(y_in, rp, rm, sa, ra, sb, rb, use):
        a_in, b_in = [], []
        for n in range(NC):
            for d in (1, 3):
                y_in[d, n].wait_recv()
            total = own[part16(n)] + rp[part16(n)].astype(F32) + rm[part16(n)].astype(F32)
            t1[part16(n)] = total
            sa[part16(n)] = total.astype(BF16)
            far = 2 if n % 2 == 0 else 14
            a_in.append(
                [
                    rcopy(
                        sa.at[pl.ds(n * 16 + ((k0 + dz) % 4) * 4, 4)],
                        ra.at[pl.ds((j * NC + n) * 4, 4)],
                        dev_z(dz),
                    )
                    for j, dz in ((2, far), (0, 1), (1, 15))
                ]
            )
        for n in range(NC):
            for copy in a_in[n]:
                copy.wait_recv()
            total = t1[pl.ds(n * 16 + k0 * 4, 4)]
            for j in range(3):
                total = total + ra[part16(j * NC + n, 4)].astype(F32)
            t1a[part16(n, 4)] = total
            sb[part16(n, 4)] = total.astype(BF16)
            b_in.append(
                [
                    rcopy(
                        sb.at[pl.ds(n * 4 + (m0 + dm) % 4, 1)],
                        rb.at[pl.ds((dm - 1) * NC + n, 1)],
                        dev_z(4 * dm),
                    )
                    for dm in (2, 1, 3)
                ]
            )
        for n in range(NC):
            for copy in b_in[n]:
                copy.wait_recv()
            total = t1a[n * 4 + m0]
            for dm in range(3):
                total = total + rb[dm * NC + n].astype(F32)
            use(n, total)

    def to_y(g, n, cls):
        rows = pl.ds(n * 64 + y * 16 + cls * 4, 4)
        return {d: rcopy(g.at[rows], g.at[rows], dev_y(d)) for d in (1, 3)}

    def gather_start(g):
        b_in = []
        for n in range(NC):
            row = pl.ds(n * 64 + y * 16 + k0 * 4 + m0, 1)
            b_in.append([rcopy(g.at[row], g.at[row], dev_z(4 * dm)) for dm in (2, 1, 3)])
        return b_in

    def gather_rest(g, b_in):
        a_in, y_in = [], []
        for n in range(NC):
            for copy in b_in[n]:
                copy.wait_recv()
            rows = pl.ds(n * 64 + y * 16 + k0 * 4, 4)
            far = 2 if n % 2 == 0 else 14
            a_in.append([rcopy(g.at[rows], g.at[rows], dev_z(dz)) for dz in (far, 1, 15)])
            y_in.append([to_y(g, n, k0)])
        for j, dk in ((1, 3), (2, 1), (0, 2)):
            for n in range(NC):
                a_in[n][j].wait_recv()
                y_in[n].append(to_y(g, n, (k0 + dk) % 4))
        return y_in

    def gather_forward(g, y_in):
        far_in = []
        for j, dk in enumerate((0, 3, 1, 2)):
            for n in range(NC):
                d = 1 if n % 2 == 0 else 3
                y_in[n][j][d].wait_recv()
                rows = pl.ds(n * 64 + ((y + 4 - d) % 4) * 16 + ((k0 + dk) % 4) * 4, 4)
                far_in.append(rcopy(g.at[rows], g.at[rows], dev_y(d)))
        return far_in

    def gather_wait(y_in, far_in, d):
        if d == 2:
            for copy in far_in:
                copy.wait_recv()
        elif d > 0:
            for n in range(NC):
                if (n % 2 == 0) != (d == 1):
                    for part in y_in[n]:
                        part[d].wait_recv()

    def gathered(g, d):
        yb = (y + 4 - d) % 4
        pieces = [
            g[pl.ds(n * 64 + yb * 16, 16)].astype(F32).reshape(128, CW).astype(BF16)
            for n in range(NC)
        ]
        return yb, jnp.concatenate(pieces, axis=1)

    def down_block(yb, put):
        for n in range(NC):
            part = jnp.dot(act_rows(yb), w[:, n * CW : (n + 1) * CW], preferred_element_type=F32)
            put(n, slice(None), part.reshape(16, 8, CW))

    y_in = rs_start(down_block, s1, f1, rp1, rm1)
    for i in range(8):
        actt[:, i * 64 : (i + 1) * 64] = act[i].astype(F32).T.astype(BF16)
    loads[2].wait()

    def use_hidden(n, total):
        hid[:, n * CW : (n + 1) * CW] = res[:, n * CW : (n + 1) * CW].astype(F32) + total

    rs_rest(y_in, rp1, rm1, s1a, ra1, s1b, rb1, use_hidden)

    mine = y * 16 + k0 * 4 + m0
    for n in range(NC):
        cols = slice(n * CW, (n + 1) * CW)
        nrm[n * 64 + mine] = (hid[:, cols] * gain_ref[:, cols]).astype(BF16)
    nrm_in = gather_start(nrm)
    h = hid[...]
    ssq[t] = jnp.broadcast_to(jnp.sum(h * h, axis=1, keepdims=True), (8, 128))
    ss_in = [rcopy(ssq.at[t], ssq.at[t], dev_t(d)) for d in (4, 3, 5, 2, 6, 1, 7)]
    for copy in ss_in:
        copy.wait_recv()
    square = ssq[0]
    for i in range(1, 8):
        square = square + ssq[i]
    inv_rms = lax.rsqrt(square / D + 1e-06)
    spot = lax.broadcasted_iota(jnp.int32, (8, 128), 1) == (
        lax.broadcasted_iota(jnp.int32, (8, 128), 0) + (k0 * 4 + m0) * 8
    )
    iv[z] = jnp.sum(jnp.where(spot, inv_rms, 0.0), axis=0, keepdims=True)
    inv_rms = inv_rms[:, :1]
    iv_in = [rcopy(iv.at[z], iv.at[z], dev_z(d)) for d in (8, 7, 9, 6, 10, 5, 11, 4, 12, 3, 13, 2, 14, 1, 15)]
    y_in = gather_rest(nrm, nrm_in)
    for copy in iv_in:
        copy.wait_recv()
    inv_row = iv[0]
    for i in range(1, NZ):
        inv_row = inv_row + iv[i]
    ivy[y] = inv_row
    ivy_in = [rcopy(ivy.at[y], ivy.at[y], dev_y(d)) for d in (2, 1, 3)]
    loads[3].wait()

    order = (0, 1, 3, 2)
    lx_at = reserve(4)
    p_in = []
    def x_copy(dx):
        return described(lx.at[(x + dx) % 4], lxr.at[dx], dev_x(dx), lx_at + dx)

    def combine(copy, row_block):
        copy.wait_recv()
        lx[row_block] = lx[row_block] + lpr[row_block]
        dx = (row_block + 4 - x) % 4

        @pl.when(dx != 0)
        def _():
            x_copy(dx).start()

    far_in = None
    blocks = []
    for d in order:
        gather_wait(y_in, far_in, d)
        yb, block = gathered(nrm, d)
        lhs[...] = block

        def columns(j, carry):
            cols = pl.ds(pl.multiple_of(j * 256, 256), 256)
            lb[:, cols] = jnp.dot(lhs[...], head[:, cols], preferred_element_type=F32)
            return carry

        lax.fori_loop(0, 5, columns, 0)

        def compact(half, dst):
            rows = pl.ds(pl.multiple_of(half * 64, 64), 64)
            mask_rows = pl.ds(pl.multiple_of(yb * 128 + half * 64, 64), 64)
            out = [jnp.zeros((64, 128), F32) for _ in range(CAP)]
            for b in range(NB):
                slot = slotb[b, mask_rows, :]
                val = lb[rows, b * BLK : (b + 1) * BLK]
                for s in range(CAP):
                    out[s] = jnp.where(slot == float(s), val, out[s])
            for s in range(CAP):
                dst[:, s * BLK : (s + 1) * BLK] = out[s]

        compact(1 - c, lp.at[yb])
        p_in.append(rcopy(lp.at[yb], lpr.at[yb], partner))
        compact(c, lx.at[yb])
        blocks.append(yb)
        if d == 0:
            far_in = gather_forward(nrm, y_in)
        if d != 1:
            while blocks:
                combine(p_in[-len(blocks)], blocks[0])
                blocks = blocks[1:]

    for copy in ivy_in:
        copy.wait_recv()
    scale_row = ivy[t // 2]
    turned = lax.broadcasted_iota(jnp.int32, (64, 128), 1) == (
        lax.broadcasted_iota(jnp.int32, (64, 128), 0) + c * 64
    )
    scale = jnp.sum(jnp.where(turned, scale_row, 0.0), axis=1, keepdims=True)
    total = lx[x]
    for dx in (1, 3, 2):
        x_copy(dx).wait_recv()
        total = total + lxr[dx]
    for dx in (1, 3, 2):
        x_copy(dx).wait_send()
    lg[...] = total * scale

    own_rows = pl.ds(pl.multiple_of(t * 64, 64), 64)
    lane = lax.broadcasted_iota(jnp.int32, (64, 128), 1)
    eye = lane == lax.broadcasted_iota(jnp.int32, (64, 128), 0)

    def to_row(col):
        return jnp.sum(jnp.where(eye, col, 0.0), axis=0, keepdims=True)

    def to_col(row):
        return jnp.sum(jnp.where(eye, row, 0.0), axis=1, keepdims=True)

    small_eye = lax.broadcasted_iota(jnp.int32, (64, 64), 0) == lax.broadcasted_iota(
        jnp.int32, (64, 64), 1
    )
    tok = jnp.sum(jnp.where(small_eye, tok_ref[...].astype(F32), 0.0), axis=1, keepdims=True)
    tok = tok.astype(jnp.int32)
    tok_block = (tok >> 7) - first_block
    tok_lane = tok & 127
    seen = jnp.zeros((64, 128), F32)
    tok_slot = jnp.full((64, 128), 99.0, F32)
    for b in range(NB):
        slot = slotb[b, own_rows, :]
        seen = seen + jnp.where(slot < 50.0, 1.0, 0.0)
        tok_slot = jnp.where(tok_block == b, slot, tok_slot)

    peak = jnp.full((64, 128), NEG, F32)
    for s in range(CAP):
        peak = jnp.maximum(peak, jnp.where(seen > float(s), lg[:, s * BLK : (s + 1) * BLK], NEG))
    peak = jnp.max(peak, axis=1, keepdims=True)
    zero = jnp.zeros((64, 128), F32)
    tot, mom, tgt = zero, zero, zero
    for s in range(CAP):
        val = lg[:, s * BLK : (s + 1) * BLK]
        ok = seen > float(s)
        shifted = jnp.where(ok, val - peak, 0.0)
        e = jnp.where(ok, jnp.exp(shifted), 0.0)
        tot = tot + e
        mom = mom + e * shifted
        tgt = tgt + jnp.where((tok_slot == float(s)) & (lane == tok_lane), val, 0.0)
    tot = jnp.sum(tot, axis=1, keepdims=True)
    mom = jnp.sum(mom, axis=1, keepdims=True)
    tgt = jnp.sum(tgt, axis=1, keepdims=True)
    stz[z] = jnp.concatenate([to_row(peak), to_row(tot), to_row(mom), to_row(tgt)], axis=0)
    st_in = [
        rcopy(stz.at[z], stz.at[z], dev_z(d))
        for d in (8, 7, 9, 6, 10, 5, 11, 4, 12, 3, 13, 2, 14, 1, 15)
    ]
    for copy in st_in:
        copy.wait_recv()

    def join(parts):
        top = parts[0][0:1]
        for p in parts[1:]:
            top = jnp.maximum(top, p[0:1])
        tot = jnp.zeros((1, 128), F32)
        mom = jnp.zeros((1, 128), F32)
        tgt = jnp.zeros((1, 128), F32)
        for p in parts:
            gap = p[0:1] - top
            scale = jnp.exp(gap)
            tot = tot + p[1:2] * scale
            mom = mom + scale * (p[2:3] + p[1:2] * gap)
            tgt = tgt + p[3:4]
        return top, tot, mom, tgt

    top, tot, mom, tgt = join([stz[i] for i in range(NZ)])
    sty[y] = jnp.concatenate([top, tot, mom, tgt], axis=0)
    y_st = [rcopy(sty.at[y], sty.at[y], dev_y(d)) for d in (2, 1, 3)]
    for copy in y_st:
        copy.wait_recv()
    top, tot, mom, tgt = join([sty[i] for i in range(NY)])
    top, tot, mom, tgt = to_col(top), to_col(tot), to_col(mom), to_col(tgt)

    response = t // 2
    length = jnp.int32(0)
    code = jnp.int32(0)
    length_sum = jnp.int32(0)
    for i in range(4):
        length = jnp.where(response == i, len_ref[i], length)
        code = jnp.where(response == i, adv_ref[i], code)
        length_sum = length_sum + len_ref[i]
    position = c * 64 + lax.broadcasted_iota(jnp.int32, (64, 1), 0)
    weight = jnp.where(position < length, code.astype(F32) / 32.0, 0.0)
    log_prob = tgt - top - jnp.log(tot)
    part = jnp.sum(weight * log_prob, axis=0, keepdims=True)
    gdot = weight * (mom / tot - (tgt - top))
    for s in range(CAP):
        val = lg[:, s * BLK : (s + 1) * BLK]
        prob = jnp.where(seen > float(s), jnp.exp(val - top), 0.0) / tot
        hot = jnp.where((tok_slot == float(s)) & (lane == tok_lane), 1.0, 0.0)
        dl[t, :, s * BLK : (s + 1) * BLK] = (weight * (prob - hot)).astype(BF16)
    dx_in = {d: rcopy(dl.at[t], dl.at[t], dev_x(d)) for d in (2, 1, 3)}
    d_in = {0: rcopy(dl.at[t], dl.at[t], partner)}
    gv[t] = to_row(gdot)
    g_in = [rcopy(gv.at[t], gv.at[t], dev_t(d)) for d in (4, 3, 5, 2, 6, 1, 7)]
    los[t] = jnp.broadcast_to(part, (8, 128))
    loss_in = [rcopy(los.at[t], los.at[t], dev_t(d)) for d in range(1, 8)]
    for d in (1, 3, 2):
        dx_in[d].wait_recv()
        slot = ((x + 4 - d) % 4) * 2 + c
        d_in[d] = rcopy(dl.at[slot], dl.at[slot], partner)
    for d in range(4):
        d_in[d].wait_recv()

    def head_block(yb, put):
        for half in range(2):
            rows = slice(half * 64, (half + 1) * 64)
            mask_rows = pl.ds(pl.multiple_of(yb * 128 + half * 64, 64), 64)
            vals = [
                dl[yb * 2 + half, :, s * BLK : (s + 1) * BLK].astype(F32) for s in range(CAP)
            ]
            for b in range(NB):
                slot = slotb[b, mask_rows, :]
                out = jnp.zeros((64, 128), F32)
                for s in range(CAP):
                    out = jnp.where(slot == float(s), vals[s], out)
                lhs2[rows, b * BLK : (b + 1) * BLK] = out.astype(BF16)
        for n in range(NC):
            for q in range(CW // 256):
                part = lax.dot_general(
                    lhs2[...],
                    head[n * CW + q * 256 : n * CW + (q + 1) * 256, :],
                    NT,
                    preferred_element_type=F32,
                )
                put(n, slice(q * 256, (q + 1) * 256), part.reshape(16, 8, 256))

    y_in = rs_start(head_block, s2, f2, rp2, rm2)
    for copy in g_in:
        copy.wait_recv()
    spot = lax.broadcasted_iota(jnp.int32, (8, 128), 1) == (
        lax.broadcasted_iota(jnp.int32, (8, 128), 0) + ((k0 % 2) * 4 + m0) * 8
    )
    gcol = jnp.sum(jnp.where(spot, gv[y * 2 + k0 // 2], 0.0), axis=1, keepdims=True)

    def use_dnormed(n, total):
        cols = slice(n * CW, (n + 1) * CW)
        value = inv_rms * (gain_ref[:, cols] * total) - hid[:, cols] * (
            inv_rms * inv_rms * gcol / D
        )
        dhg[n * 64 + mine] = value.astype(BF16)

    rs_rest(y_in, rp2, rm2, s2a, ra2, s2b, rb2, use_dnormed)
    y_in = gather_rest(dhg, gather_start(dhg))

    ag_in = {}
    far_in = None
    for d in order:
        gather_wait(y_in, far_in, d)
        yb, block = gathered(dhg, d)
        dh[pl.ds(pl.multiple_of(yb * 128, 128), 128), :] = block
        part_a = lax.dot_general(block, w[...], NT, preferred_element_type=F32)
        ags[2 * yb] = part_a[:64]
        ags[2 * yb + 1] = part_a[64:]
        agr[2 * yb] = part_a[:64].astype(BF16)
        agr[2 * yb + 1] = part_a[64:].astype(BF16)
        if d == order[0]:
            far_in = gather_forward(dhg, y_in)
    for d in (4, 3, 5, 2, 6, 1, 7):
        ag_in[d] = rcopy(agr.at[(t + d) % 8], agr.at[8 + d], dev_t(d))
    for copy in loss_in:
        copy.wait_recv()
    objective = los[0]
    for i in range(1, 8):
        objective = objective + los[i]
    loss_ref[...] = -objective / length_sum.astype(F32)
    total = ags[t]
    for d in range(1, 8):
        ag_in[d].wait_recv()
        total = total + agr[8 + d].astype(F32)
    ag_ref[...] = total.astype(BF16)
    for copy in sends:
        copy.wait_send()


def last(actt, dh, ag, loss, loss_ref, dg_ref, ag_ref):
    dg_ref[...] = jnp.dot(actt[...], dh[...], preferred_element_type=F32).astype(BF16)
    ag_ref[...] = ag[...]
    loss_ref[...] = loss[0:1, 0:1]


def body(
    residual,
    activation,
    down_weight,
    norm_gain,
    head_weight,
    allowed,
    tokens,
    lengths,
    advantage_code,
):
    any_spec = pl.BlockSpec(memory_space=pl.ANY)
    vmem = pl.BlockSpec(memory_space=pltpu.VMEM)
    smem = pl.BlockSpec(memory_space=pltpu.SMEM)
    v = pltpu.VMEM
    out = pl.pallas_call(
        kernel,
        out_shape=(
            jax.ShapeDtypeStruct((256, 512), BF16),
            jax.ShapeDtypeStruct((512, 1024), BF16),
            jax.ShapeDtypeStruct((64, 256), BF16),
            jax.ShapeDtypeStruct((8, 128), F32),
        ),
        in_specs=[any_spec, any_spec, any_spec, vmem, any_spec, vmem, vmem, smem, smem],
        out_specs=(vmem, vmem, vmem, vmem),
        scratch_shapes=[
            v((8, 1024), BF16),
            v((8, 64, 256), BF16),
            v((256, 1024), BF16),
            v((1024, 1280), BF16),
            v((NB, 512, 128), F32),
            v((NC * 16, 8, CW), F32),
            v((NC * 16, 8, CW), F32),
            v((NC * 64, 8, CW), BF16),
            v((NC * 16, 8, CW), BF16),
            v((NC * 16, 8, CW), BF16),
            v((NC * 16, 8, CW), BF16),
            v((NC * 16, 8, CW), F32),
            v((NC * 16, 8, CW), BF16),
            v((3 * NC * 4, 8, CW), BF16),
            v((NC * 4, 8, CW), F32),
            v((NC * 4, 8, CW), BF16),
            v((3 * NC, 8, CW), BF16),
            v((8, 1024), F32),
            v((8, 8, 128), F32),
            v((NZ, 1, 128), F32),
            v((NY, 1, 128), F32),
            v((NC * 64, 8, CW), BF16),
            v((NC * 64, 8, CW), BF16),
            v((NC * 16, 8, CW), BF16),
            v((NC * 16, 8, CW), BF16),
            v((NC * 16, 8, CW), BF16),
            v((NC * 16, 8, CW), BF16),
            v((3 * NC * 4, 8, CW), BF16),
            v((NC * 4, 8, CW), BF16),
            v((3 * NC, 8, CW), BF16),
            v((NC * 64, 8, CW), BF16),
            v((128, 1024), BF16),
            v((128, 1280), F32),
            v((4, 64, CAP * BLK), F32),
            v((4, 64, CAP * BLK), F32),
            v((4, 64, CAP * BLK), F32),
            v((4, 64, CAP * BLK), F32),
            v((64, CAP * BLK), F32),
            v((NZ, 4, 128), F32),
            v((NY, 4, 128), F32),
            v((8, 64, CAP * BLK), BF16),
            v((8, 1, 128), F32),
            v((128, 1280), BF16),
            v((8, 64, 256), F32),
            v((16, 64, 256), BF16),
            v((8, 8, 128), F32),
            pltpu.SemaphoreType.DMA((4,)),
            pltpu.SemaphoreType.DMA((N_SEND,)),
            pltpu.SemaphoreType.DMA((N_SEND,)),
        ],
        compiler_params=pltpu.CompilerParams(
            collective_id=0, has_side_effects=True, vmem_limit_bytes=60 * 1024 * 1024
        ),
        name="step",
    )(
        residual.reshape(64, 8, 1024),
        activation,
        down_weight,
        norm_gain.reshape(1, 1024),
        head_weight,
        allowed.T,
        tokens.reshape(1, 64),
        lengths,
        advantage_code,
    )
    loss, dg, ag = pl.pallas_call(
        last,
        out_shape=(
            jax.ShapeDtypeStruct((1, 1), F32),
            jax.ShapeDtypeStruct((256, 1024), BF16),
            jax.ShapeDtypeStruct((64, 256), BF16),
        ),
        in_specs=[vmem] * 4,
        out_specs=(vmem, vmem, vmem),
        name="last",
    )(*out)
    return loss.reshape(()), dg, ag


def solution(mesh):
    in_specs = (
        P(None, "tp"),
        P("tp", "vocab"),
        P("vocab", "tp"),
        P("tp"),
        P("tp", "vocab"),
        P(),
        P("tp"),
        P(),
        P(),
    )
    out_specs = (P(), P("vocab", "tp"), P("tp", "vocab"))
    return jax.shard_map(body, mesh=mesh, in_specs=in_specs, out_specs=out_specs, check_vma=False)
```

```python
import jax
import jax.numpy as jnp
from jax import lax
from jax.experimental import pallas as pl
from jax.experimental.pallas import tpu as pltpu
from jax.sharding import PartitionSpec as P

MESH = pl.DeviceIdType.MESH
F32 = jnp.float32
BF16 = jnp.bfloat16
D = 8192
BLK = 128
CAP = 4
NB = 10
NY = 4
NZ = 16
NX = 4
NEG = -1e30
NC = 4
CW = 1024 // NC
N_SEND = 330
NT = (((1,), (1,)), ((), ()))


def kernel(
    res_hbm,
    act_hbm,
    w_hbm,
    gain_ref,
    head_hbm,
    allowed_ref,
    tok_ref,
    len_ref,
    adv_ref,
    actt,
    dh,
    ag_ref,
    loss_ref,
    res,
    act,
    w,
    head,
    slotb,
    own,
    fo,
    s1,
    f1,
    rp1,
    rm1,
    t1,
    s1a,
    ra1,
    t1a,
    t1b,
    rb1,
    hid,
    ssq,
    iv,
    ivy,
    nrm,
    s2,
    f2,
    rp2,
    rm2,
    s2a,
    ra2,
    s2b,
    rb2,
    dhg,
    lhs,
    lb,
    lp,
    lpr,
    lx,
    lxr,
    lg,
    stz,
    sty,
    dl,
    gv,
    lhs2,
    ags,
    agr,
    los,
    lsem,
    ssem,
    rsem,
):
    v = lax.axis_index("vocab")
    t = lax.axis_index("tp")
    y = v // NZ
    z = v % NZ
    x = t // 2
    c = t % 2
    k0 = z % 4
    m0 = z // 4

    def dev_y(d):
        return (((y + d) % NY) * NZ + z, t)

    def dev_z(d):
        return (y * NZ + (z + d) % NZ, t)

    def dev_t(d):
        return (v, (t + d) % 8)

    def dev_x(d):
        return (v, ((x + d) % NX) * 2 + c)

    partner = (v, x * 2 + (1 - c))

    barrier = pltpu.get_barrier_semaphore()
    peers = (
        [dev_t(d) for d in range(1, 8)]
        + [dev_y(d) for d in range(1, 4)]
        + [dev_z(d) for d in range(1, NZ)]
    )
    for dev in peers:
        pl.semaphore_signal(barrier, inc=1, device_id=dev, device_id_type=MESH)

    loads = [
        pltpu.make_async_copy(act_hbm, act.at[t], lsem.at[0]),
        pltpu.make_async_copy(w_hbm, w, lsem.at[1]),
        pltpu.make_async_copy(res_hbm.at[y * 16 + k0 * 4 + m0], res, lsem.at[2]),
        pltpu.make_async_copy(head_hbm, head, lsem.at[3]),
    ]
    for copy in loads:
        copy.start()

    first_block = v * NB

    def prep(i, carry):
        rows = pl.ds(pl.multiple_of(i * 128, 128), 128)
        listed = allowed_ref[:, rows]
        run = jnp.zeros((1, 128), F32)
        slots = []
        for b in range(NB):
            hit = jnp.max(
                jnp.where(listed == first_block + b, 1.0, 0.0).astype(F32), axis=0, keepdims=True
            )
            slots.append(jnp.where(hit > 0.5, run, 99.0))
            run = run + hit
        turned = jnp.concatenate(slots + [jnp.zeros((128 - NB, 128), F32)], axis=0).T
        for b in range(NB):
            slotb[b, rows, :] = jnp.broadcast_to(turned[:, b : b + 1], (128, 128))
        return carry

    lax.fori_loop(0, 4, prep, 0)

    sends = []
    count = [0]

    def rcopy(src, dst, dev):
        i = count[0]
        count[0] += 1
        copy = pltpu.make_async_remote_copy(
            src_ref=src,
            dst_ref=dst,
            send_sem=ssem.at[i],
            recv_sem=rsem.at[i],
            device_id=dev,
            device_id_type=MESH,
        )
        copy.start()
        sends.append(copy)
        return copy

    def reserve(k):
        i = count[0]
        count[0] += k
        return i

    def described(src, dst, dev, i):
        return pltpu.make_async_remote_copy(
            src_ref=src,
            dst_ref=dst,
            send_sem=ssem.at[i],
            recv_sem=rsem.at[i],
            device_id=dev,
            device_id_type=MESH,
        )

    loads[0].wait()
    pl.semaphore_wait(barrier, len(peers))

    a_in = [rcopy(act.at[t], act.at[t], dev_t(d)) for d in (4, 3, 5, 2, 6, 1, 7)]
    loads[1].wait()
    for copy in a_in:
        copy.wait_recv()

    def act_rows(yb):
        return jnp.concatenate([act[2 * yb], act[2 * yb + 1]], axis=0)

    def part16(n, k=16):
        return slice(n * k, (n + 1) * k)

    def rs_start(block, s, f, rp, rm):
        step_one, step_two = {}, {}
        far = (y + 2) % 4
        block(far, lambda n, cols, part: s.__setitem__(
            (pl.ds(n * 64 + far * 16, 16), slice(None), cols), part.astype(BF16)))
        for n in range(NC):
            step_one[n] = rcopy(
                s.at[pl.ds(n * 64 + far * 16, 16)],
                f.at[pl.ds(n * 16, 16)],
                dev_y(1 if n % 2 == 0 else 3),
            )
        for d in (1, 3):
            yb = (y + d) % 4

            def put(n, cols, part, d=d, yb=yb):
                if (n % 2 == 0) == (d == 1):
                    fo[part16(n), :, cols] = part
                else:
                    s[pl.ds(n * 64 + yb * 16, 16), :, cols] = part.astype(BF16)

            block(yb, put)

        def put_own(n, cols, part):
            own[part16(n), :, cols] = part

        def send(n, d):
            rows = pl.ds(n * 64 + ((y + d) % 4) * 16, 16)
            step_two[d, n] = rcopy(
                s.at[rows], (rp if d == 1 else rm).at[pl.ds(n * 16, 16)], dev_y(d)
            )

        for first in range(0, NC, 2):
            send(first, 3)
            send(first + 1, 1)
            if first == 0:
                block(y, put_own)
            for n, d in ((first, 1), (first + 1, 3)):
                rows = pl.ds(n * 64 + ((y + d) % 4) * 16, 16)
                step_one[n].wait_recv()
                s[rows] = (fo[part16(n)] + f[part16(n)].astype(F32)).astype(BF16)
                send(n, d)
        return step_two

    def rs_rest(y_in, rp, rm, sa, ra, ta, sb, rb, use):
        a_in, b_in = [], []
        for n in range(NC):
            for d in (1, 3):
                y_in[d, n].wait_recv()
            total = own[part16(n)] + rp[part16(n)].astype(F32) + rm[part16(n)].astype(F32)
            t1[part16(n)] = total
            sa[part16(n)] = total.astype(BF16)
            far = 2 if n % 2 == 0 else 14
            a_in.append(
                [
                    rcopy(
                        sa.at[pl.ds(n * 16 + ((k0 + dz) % 4) * 4, 4)],
                        ra.at[pl.ds((j * NC + n) * 4, 4)],
                        dev_z(dz),
                    )
                    for j, dz in ((2, far), (0, 1), (1, 15))
                ]
            )
        for n in range(NC):
            for copy in a_in[n]:
                copy.wait_recv()
            total = t1[pl.ds(n * 16 + k0 * 4, 4)]
            for j in range(3):
                total = total + ra[part16(j * NC + n, 4)].astype(F32)
            ta[part16(n, 4)] = total
            if sb is not ta:
                sb[part16(n, 4)] = total.astype(BF16)
            b_in.append(
                [
                    rcopy(
                        sb.at[pl.ds(n * 4 + (m0 + dm) % 4, 1)],
                        rb.at[pl.ds((dm - 1) * NC + n, 1)],
                        dev_z(4 * dm),
                    )
                    for dm in (2, 1, 3)
                ]
            )
        for n in range(NC):
            for copy in b_in[n]:
                copy.wait_recv()
            total = ta[n * 4 + m0]
            for dm in range(3):
                total = total + rb[dm * NC + n].astype(F32)
            use(n, total)

    def piece(dy, dz):
        zz = (z + dz) % NZ
        return pl.ds(((y + dy) % NY) * 16 + (zz % 4) * 4 + zz // 4, 1)

    class Gather:
        def __init__(self, g):
            self.g = g
            self.order = []
            self.y_in = []
            self.far_in = []
            self.z_in = {d: self.send(0, 0, dev_z(d)) for d in (8, 4, 12, 2, 14, 1, 15)}
            self.to_y(0)

        def send(self, dy, dz, dev):
            ref = self.g.at[piece(dy, dz)]
            return rcopy(ref, ref, dev)

        def to_y(self, dz):
            self.order.append(dz)
            self.y_in.append({d: self.send(0, dz, dev_y(d)) for d in (1, 3)})

        def arrived(self, copy, dz):
            copy.wait_recv()
            self.to_y(dz)

        def near(self):
            for d, dz in ((1, 15), (15, 1), (2, 14), (14, 2)):
                self.arrived(self.z_in[d], dz)

        def distant(self):
            self.z_in[4].wait_recv()
            low = [self.send(0, 12, dev_z(d)) for d in (1, 15, 2)]
            self.to_y(12)
            self.z_in[12].wait_recv()
            high = [self.send(0, 4, dev_z(d)) for d in (1, 15, 14)]
            self.to_y(4)
            self.forward(5)
            for copy, dz in ((low[0], 11), (high[0], 3), (low[1], 13), (high[1], 5)):
                self.arrived(copy, dz)
            self.z_in[8].wait_recv()
            across = [self.send(0, 8, dev_z(d)) for d in (1, 15)]
            self.to_y(8)
            self.arrived(low[2], 10)
            self.arrived(high[2], 6)
            self.forward(7)
            self.arrived(across[0], 7)
            self.arrived(across[1], 9)

        def forward(self, upto=16):
            for j in range(len(self.far_in), upto):
                d = 1 if j % 2 == 0 else 3
                self.y_in[j][d].wait_recv()
                self.far_in.append(self.send(4 - d, self.order[j], dev_y(d)))

        def wait(self, d):
            if d == 2:
                for copy in self.far_in:
                    copy.wait_recv()
            elif d > 0:
                for j in range(16):
                    if (j % 2 == 0) != (d == 1):
                        self.y_in[j][d].wait_recv()

        def block(self, d):
            yb = (y + 4 - d) % 4
            rows = self.g[pl.ds(yb * 16, 16)]
            return yb, rows.astype(F32).reshape(128, 1024).astype(BF16)

    def down_block(yb, put):
        for n in range(NC):
            part = jnp.dot(act_rows(yb), w[:, n * CW : (n + 1) * CW], preferred_element_type=F32)
            put(n, slice(None), part.reshape(16, 8, CW))

    y_in = rs_start(down_block, s1, f1, rp1, rm1)
    for i in range(8):
        actt[:, i * 64 : (i + 1) * 64] = act[i].astype(F32).T.astype(BF16)
    loads[2].wait()

    def use_hidden(n, total):
        hid[:, n * CW : (n + 1) * CW] = res[:, n * CW : (n + 1) * CW].astype(F32) + total

    rs_rest(y_in, rp1, rm1, s1a, ra1, t1a, t1a, rb1, use_hidden)

    mine = y * 16 + k0 * 4 + m0
    nrm[mine] = (hid[...] * gain_ref[...]).astype(BF16)
    nrm_all = Gather(nrm)
    h = hid[...]
    ssq[t] = jnp.broadcast_to(jnp.sum(h * h, axis=1, keepdims=True), (8, 128))
    ss_in = [rcopy(ssq.at[t], ssq.at[t], dev_t(d)) for d in (4, 3, 5, 2, 6, 1, 7)]
    nrm_all.near()
    for copy in ss_in:
        copy.wait_recv()
    square = ssq[0]
    for i in range(1, 8):
        square = square + ssq[i]
    inv_rms = lax.rsqrt(square / D + 1e-06)
    spot = lax.broadcasted_iota(jnp.int32, (8, 128), 1) == (
        lax.broadcasted_iota(jnp.int32, (8, 128), 0) + (k0 * 4 + m0) * 8
    )
    iv[z] = jnp.sum(jnp.where(spot, inv_rms, 0.0), axis=0, keepdims=True)
    inv_rms = inv_rms[:, :1]
    iv_in = [rcopy(iv.at[z], iv.at[z], dev_z(d)) for d in (8, 7, 9, 6, 10, 5, 11, 4, 12, 3, 13, 2, 14, 1, 15)]
    nrm_all.distant()
    for copy in iv_in:
        copy.wait_recv()
    inv_row = iv[0]
    for i in range(1, NZ):
        inv_row = inv_row + iv[i]
    ivy[y] = inv_row
    ivy_in = [rcopy(ivy.at[y], ivy.at[y], dev_y(d)) for d in (2, 1, 3)]
    loads[3].wait()

    order = (0, 1, 3, 2)
    lx_at = reserve(4)
    p_in = []
    def x_copy(dx):
        return described(lx.at[(x + dx) % 4], lxr.at[dx], dev_x(dx), lx_at + dx)

    def combine(copy, row_block):
        copy.wait_recv()
        lx[row_block] = lx[row_block] + lpr[row_block]
        dx = (row_block + 4 - x) % 4

        @pl.when(dx != 0)
        def _():
            x_copy(dx).start()

    blocks = []
    for d in order:
        nrm_all.wait(d)
        yb, block = nrm_all.block(d)
        lhs[...] = block

        def columns(j, carry):
            cols = pl.ds(pl.multiple_of(j * 256, 256), 256)
            lb[:, cols] = jnp.dot(lhs[...], head[:, cols], preferred_element_type=F32)
            return carry

        lax.fori_loop(0, 5, columns, 0)

        def compact(half, dst):
            rows = pl.ds(pl.multiple_of(half * 64, 64), 64)
            mask_rows = pl.ds(pl.multiple_of(yb * 128 + half * 64, 64), 64)
            out = [jnp.zeros((64, 128), F32) for _ in range(CAP)]
            for b in range(NB):
                slot = slotb[b, mask_rows, :]
                val = lb[rows, b * BLK : (b + 1) * BLK]
                for s in range(CAP):
                    out[s] = jnp.where(slot == float(s), val, out[s])
            for s in range(CAP):
                dst[:, s * BLK : (s + 1) * BLK] = out[s]

        compact(1 - c, lp.at[yb])
        p_in.append(rcopy(lp.at[yb], lpr.at[yb], partner))
        compact(c, lx.at[yb])
        blocks.append(yb)
        if d == 0:
            nrm_all.forward()
        if d != 1:
            while blocks:
                combine(p_in[-len(blocks)], blocks[0])
                blocks = blocks[1:]

    for copy in ivy_in:
        copy.wait_recv()
    scale_row = ivy[t // 2]
    turned = lax.broadcasted_iota(jnp.int32, (64, 128), 1) == (
        lax.broadcasted_iota(jnp.int32, (64, 128), 0) + c * 64
    )
    scale = jnp.sum(jnp.where(turned, scale_row, 0.0), axis=1, keepdims=True)
    total = lx[x]
    for dx in (1, 3, 2):
        x_copy(dx).wait_recv()
        total = total + lxr[dx]
    for dx in (1, 3, 2):
        x_copy(dx).wait_send()
    lg[...] = total * scale

    own_rows = pl.ds(pl.multiple_of(t * 64, 64), 64)
    lane = lax.broadcasted_iota(jnp.int32, (64, 128), 1)
    eye = lane == lax.broadcasted_iota(jnp.int32, (64, 128), 0)

    def to_row(col):
        return jnp.sum(jnp.where(eye, col, 0.0), axis=0, keepdims=True)

    def to_col(row):
        return jnp.sum(jnp.where(eye, row, 0.0), axis=1, keepdims=True)

    small_eye = lax.broadcasted_iota(jnp.int32, (64, 64), 0) == lax.broadcasted_iota(
        jnp.int32, (64, 64), 1
    )
    tok = jnp.sum(jnp.where(small_eye, tok_ref[...].astype(F32), 0.0), axis=1, keepdims=True)
    tok = tok.astype(jnp.int32)
    tok_block = (tok >> 7) - first_block
    tok_lane = tok & 127
    seen = jnp.zeros((64, 128), F32)
    tok_slot = jnp.full((64, 128), 99.0, F32)
    for b in range(NB):
        slot = slotb[b, own_rows, :]
        seen = seen + jnp.where(slot < 50.0, 1.0, 0.0)
        tok_slot = jnp.where(tok_block == b, slot, tok_slot)

    peak = jnp.full((64, 128), NEG, F32)
    for s in range(CAP):
        peak = jnp.maximum(peak, jnp.where(seen > float(s), lg[:, s * BLK : (s + 1) * BLK], NEG))
    peak = jnp.max(peak, axis=1, keepdims=True)
    zero = jnp.zeros((64, 128), F32)
    tot, mom, tgt = zero, zero, zero
    for s in range(CAP):
        val = lg[:, s * BLK : (s + 1) * BLK]
        ok = seen > float(s)
        shifted = jnp.where(ok, val - peak, 0.0)
        e = jnp.where(ok, jnp.exp(shifted), 0.0)
        tot = tot + e
        mom = mom + e * shifted
        tgt = tgt + jnp.where((tok_slot == float(s)) & (lane == tok_lane), val, 0.0)
    tot = jnp.sum(tot, axis=1, keepdims=True)
    mom = jnp.sum(mom, axis=1, keepdims=True)
    tgt = jnp.sum(tgt, axis=1, keepdims=True)
    stz[z] = jnp.concatenate([to_row(peak), to_row(tot), to_row(mom), to_row(tgt)], axis=0)
    st_in = [
        rcopy(stz.at[z], stz.at[z], dev_z(d))
        for d in (8, 7, 9, 6, 10, 5, 11, 4, 12, 3, 13, 2, 14, 1, 15)
    ]
    for copy in st_in:
        copy.wait_recv()

    def join(parts):
        top = parts[0][0:1]
        for p in parts[1:]:
            top = jnp.maximum(top, p[0:1])
        tot = jnp.zeros((1, 128), F32)
        mom = jnp.zeros((1, 128), F32)
        tgt = jnp.zeros((1, 128), F32)
        for p in parts:
            gap = p[0:1] - top
            scale = jnp.exp(gap)
            tot = tot + p[1:2] * scale
            mom = mom + scale * (p[2:3] + p[1:2] * gap)
            tgt = tgt + p[3:4]
        return top, tot, mom, tgt

    top, tot, mom, tgt = join([stz[i] for i in range(NZ)])
    sty[y] = jnp.concatenate([top, tot, mom, tgt], axis=0)
    y_st = [rcopy(sty.at[y], sty.at[y], dev_y(d)) for d in (2, 1, 3)]
    for copy in y_st:
        copy.wait_recv()
    top, tot, mom, tgt = join([sty[i] for i in range(NY)])
    top, tot, mom, tgt = to_col(top), to_col(tot), to_col(mom), to_col(tgt)

    response = t // 2
    length = jnp.int32(0)
    code = jnp.int32(0)
    length_sum = jnp.int32(0)
    for i in range(4):
        length = jnp.where(response == i, len_ref[i], length)
        code = jnp.where(response == i, adv_ref[i], code)
        length_sum = length_sum + len_ref[i]
    position = c * 64 + lax.broadcasted_iota(jnp.int32, (64, 1), 0)
    weight = jnp.where(position < length, code.astype(F32) / 32.0, 0.0)
    log_prob = tgt - top - jnp.log(tot)
    part = jnp.sum(weight * log_prob, axis=0, keepdims=True)
    gdot = weight * (mom / tot - (tgt - top))
    for s in range(CAP):
        val = lg[:, s * BLK : (s + 1) * BLK]
        prob = jnp.where(seen > float(s), jnp.exp(val - top), 0.0) / tot
        hot = jnp.where((tok_slot == float(s)) & (lane == tok_lane), 1.0, 0.0)
        dl[t, :, s * BLK : (s + 1) * BLK] = (weight * (prob - hot)).astype(BF16)
    dx_in = {d: rcopy(dl.at[t], dl.at[t], dev_x(d)) for d in (2, 1, 3)}
    d_in = {0: rcopy(dl.at[t], dl.at[t], partner)}
    gv[t] = to_row(gdot)
    g_in = [rcopy(gv.at[t], gv.at[t], dev_t(d)) for d in (4, 3, 5, 2, 6, 1, 7)]
    los[t] = jnp.broadcast_to(part, (8, 128))
    loss_in = [rcopy(los.at[t], los.at[t], dev_t(d)) for d in range(1, 8)]
    for d in (1, 3, 2):
        dx_in[d].wait_recv()
        slot = ((x + 4 - d) % 4) * 2 + c
        d_in[d] = rcopy(dl.at[slot], dl.at[slot], partner)
    for d in range(4):
        d_in[d].wait_recv()

    def head_block(yb, put):
        for half in range(2):
            rows = slice(half * 64, (half + 1) * 64)
            mask_rows = pl.ds(pl.multiple_of(yb * 128 + half * 64, 64), 64)
            vals = [
                dl[yb * 2 + half, :, s * BLK : (s + 1) * BLK].astype(F32) for s in range(CAP)
            ]
            for b in range(NB):
                slot = slotb[b, mask_rows, :]
                out = jnp.zeros((64, 128), F32)
                for s in range(CAP):
                    out = jnp.where(slot == float(s), vals[s], out)
                lhs2[rows, b * BLK : (b + 1) * BLK] = out.astype(BF16)
        for n in range(NC):
            for q in range(CW // 256):
                part = lax.dot_general(
                    lhs2[...],
                    head[n * CW + q * 256 : n * CW + (q + 1) * 256, :],
                    NT,
                    preferred_element_type=F32,
                )
                put(n, slice(q * 256, (q + 1) * 256), part.reshape(16, 8, 256))

    y_in = rs_start(head_block, s2, f2, rp2, rm2)
    for copy in g_in:
        copy.wait_recv()
    spot = lax.broadcasted_iota(jnp.int32, (8, 128), 1) == (
        lax.broadcasted_iota(jnp.int32, (8, 128), 0) + ((k0 % 2) * 4 + m0) * 8
    )
    gcol = jnp.sum(jnp.where(spot, gv[y * 2 + k0 // 2], 0.0), axis=1, keepdims=True)

    def use_dnormed(n, total):
        cols = slice(n * CW, (n + 1) * CW)
        value = inv_rms * (gain_ref[:, cols] * total) - hid[:, cols] * (
            inv_rms * inv_rms * gcol / D
        )
        dhg[mine, :, cols] = value.astype(BF16)

    rs_rest(y_in, rp2, rm2, s2a, ra2, t1b, s2b, rb2, use_dnormed)
    dhg_all = Gather(dhg)
    dhg_all.near()
    dhg_all.distant()

    ag_in = {}
    for d in order:
        dhg_all.wait(d)
        yb, block = dhg_all.block(d)
        dh[pl.ds(pl.multiple_of(yb * 128, 128), 128), :] = block
        part_a = lax.dot_general(block, w[...], NT, preferred_element_type=F32)
        ags[2 * yb] = part_a[:64]
        ags[2 * yb + 1] = part_a[64:]
        agr[2 * yb] = part_a[:64].astype(BF16)
        agr[2 * yb + 1] = part_a[64:].astype(BF16)
        if d == order[0]:
            dhg_all.forward()
    for d in (4, 3, 5, 2, 6, 1, 7):
        ag_in[d] = rcopy(agr.at[(t + d) % 8], agr.at[8 + d], dev_t(d))
    for copy in loss_in:
        copy.wait_recv()
    objective = los[0]
    for i in range(1, 8):
        objective = objective + los[i]
    loss_ref[...] = -objective / length_sum.astype(F32)
    total = ags[t]
    for d in range(1, 8):
        ag_in[d].wait_recv()
        total = total + agr[8 + d].astype(F32)
    ag_ref[...] = total.astype(BF16)
    for copy in sends:
        copy.wait_send()


def last(actt, dh, ag, loss, loss_ref, dg_ref, ag_ref):
    dg_ref[...] = jnp.dot(actt[...], dh[...], preferred_element_type=F32).astype(BF16)
    ag_ref[...] = ag[...]
    loss_ref[...] = loss[0:1, 0:1]


def body(
    residual,
    activation,
    down_weight,
    norm_gain,
    head_weight,
    allowed,
    tokens,
    lengths,
    advantage_code,
):
    any_spec = pl.BlockSpec(memory_space=pl.ANY)
    vmem = pl.BlockSpec(memory_space=pltpu.VMEM)
    smem = pl.BlockSpec(memory_space=pltpu.SMEM)
    v = pltpu.VMEM
    out = pl.pallas_call(
        kernel,
        out_shape=(
            jax.ShapeDtypeStruct((256, 512), BF16),
            jax.ShapeDtypeStruct((512, 1024), BF16),
            jax.ShapeDtypeStruct((64, 256), BF16),
            jax.ShapeDtypeStruct((8, 128), F32),
        ),
        in_specs=[any_spec, any_spec, any_spec, vmem, any_spec, vmem, vmem, smem, smem],
        out_specs=(vmem, vmem, vmem, vmem),
        scratch_shapes=[
            v((8, 1024), BF16),
            v((8, 64, 256), BF16),
            v((256, 1024), BF16),
            v((1024, 1280), BF16),
            v((NB, 512, 128), F32),
            v((NC * 16, 8, CW), F32),
            v((NC * 16, 8, CW), F32),
            v((NC * 64, 8, CW), BF16),
            v((NC * 16, 8, CW), BF16),
            v((NC * 16, 8, CW), BF16),
            v((NC * 16, 8, CW), BF16),
            v((NC * 16, 8, CW), F32),
            v((NC * 16, 8, CW), BF16),
            v((3 * NC * 4, 8, CW), BF16),
            v((NC * 4, 8, CW), F32),
            v((NC * 4, 8, CW), F32),
            v((3 * NC, 8, CW), F32),
            v((8, 1024), F32),
            v((8, 8, 128), F32),
            v((NZ, 1, 128), F32),
            v((NY, 1, 128), F32),
            v((64, 8, 1024), BF16),
            v((NC * 64, 8, CW), BF16),
            v((NC * 16, 8, CW), BF16),
            v((NC * 16, 8, CW), BF16),
            v((NC * 16, 8, CW), BF16),
            v((NC * 16, 8, CW), BF16),
            v((3 * NC * 4, 8, CW), BF16),
            v((NC * 4, 8, CW), BF16),
            v((3 * NC, 8, CW), BF16),
            v((64, 8, 1024), BF16),
            v((128, 1024), BF16),
            v((128, 1280), F32),
            v((4, 64, CAP * BLK), F32),
            v((4, 64, CAP * BLK), F32),
            v((4, 64, CAP * BLK), F32),
            v((4, 64, CAP * BLK), F32),
            v((64, CAP * BLK), F32),
            v((NZ, 4, 128), F32),
            v((NY, 4, 128), F32),
            v((8, 64, CAP * BLK), BF16),
            v((8, 1, 128), F32),
            v((128, 1280), BF16),
            v((8, 64, 256), F32),
            v((16, 64, 256), BF16),
            v((8, 8, 128), F32),
            pltpu.SemaphoreType.DMA((4,)),
            pltpu.SemaphoreType.DMA((N_SEND,)),
            pltpu.SemaphoreType.DMA((N_SEND,)),
        ],
        compiler_params=pltpu.CompilerParams(
            collective_id=0, has_side_effects=True, vmem_limit_bytes=60 * 1024 * 1024
        ),
        name="step",
    )(
        residual.reshape(64, 8, 1024),
        activation,
        down_weight,
        norm_gain.reshape(1, 1024),
        head_weight,
        allowed.T,
        tokens.reshape(1, 64),
        lengths,
        advantage_code,
    )
    loss, dg, ag = pl.pallas_call(
        last,
        out_shape=(
            jax.ShapeDtypeStruct((1, 1), F32),
            jax.ShapeDtypeStruct((256, 1024), BF16),
            jax.ShapeDtypeStruct((64, 256), BF16),
        ),
        in_specs=[vmem] * 4,
        out_specs=(vmem, vmem, vmem),
        name="last",
    )(*out)
    return loss.reshape(()), dg, ag


def solution(mesh):
    in_specs = (
        P(None, "tp"),
        P("tp", "vocab"),
        P("vocab", "tp"),
        P("tp"),
        P("tp", "vocab"),
        P(),
        P("tp"),
        P(),
        P(),
    )
    out_specs = (P(), P("vocab", "tp"), P("tp", "vocab"))
    return jax.shard_map(body, mesh=mesh, in_specs=in_specs, out_specs=out_specs, check_vma=False)
```

```python
import jax
import jax.numpy as jnp
from jax import lax
from jax.experimental import pallas as pl
from jax.experimental.pallas import tpu as pltpu
from jax.sharding import PartitionSpec as P

MESH = pl.DeviceIdType.MESH
F32 = jnp.float32
BF16 = jnp.bfloat16
D = 8192
BLK = 128
CAP = 4
NB = 10
NY = 4
NZ = 16
NX = 4
NEG = -1e30
NC = 4
CW = 1024 // NC
N_SEND = 330
NT = (((1,), (1,)), ((), ()))


def kernel(
    res_hbm,
    act_hbm,
    w_hbm,
    gain_ref,
    head_hbm,
    allowed_ref,
    tok_ref,
    len_ref,
    adv_ref,
    dg_ref,
    ag_ref,
    loss_ref,
    actt,
    dh,
    res,
    act,
    w,
    head,
    slotb,
    own,
    fo,
    s1,
    f1,
    rp1,
    rm1,
    t1,
    s1a,
    ra1,
    t1a,
    t1b,
    rb1,
    hid,
    ssq,
    iv,
    ivy,
    nrm,
    s2,
    f2,
    rp2,
    rm2,
    s2a,
    ra2,
    s2b,
    rb2,
    dhg,
    lhs,
    lb,
    lp,
    lpr,
    lx,
    lxr,
    lg,
    stz,
    sty,
    dl,
    gv,
    lhs2,
    ags,
    agr,
    los,
    lsem,
    ssem,
    rsem,
):
    v = lax.axis_index("vocab")
    t = lax.axis_index("tp")
    y = v // NZ
    z = v % NZ
    x = t // 2
    c = t % 2
    k0 = z % 4
    m0 = z // 4

    def dev_y(d):
        return (((y + d) % NY) * NZ + z, t)

    def dev_z(d):
        return (y * NZ + (z + d) % NZ, t)

    def dev_t(d):
        return (v, (t + d) % 8)

    def dev_x(d):
        return (v, ((x + d) % NX) * 2 + c)

    partner = (v, x * 2 + (1 - c))

    barrier = pltpu.get_barrier_semaphore()
    peers = (
        [dev_t(d) for d in range(1, 8)]
        + [dev_y(d) for d in range(1, 4)]
        + [dev_z(d) for d in range(1, NZ)]
    )
    for dev in peers:
        pl.semaphore_signal(barrier, inc=1, device_id=dev, device_id_type=MESH)

    loads = [
        pltpu.make_async_copy(act_hbm, act.at[t], lsem.at[0]),
        pltpu.make_async_copy(w_hbm, w, lsem.at[1]),
        pltpu.make_async_copy(res_hbm.at[y * 16 + k0 * 4 + m0], res, lsem.at[2]),
        pltpu.make_async_copy(head_hbm, head, lsem.at[3]),
    ]
    for copy in loads:
        copy.start()

    first_block = v * NB

    def prep(i, carry):
        rows = pl.ds(pl.multiple_of(i * 128, 128), 128)
        listed = allowed_ref[:, rows]
        run = jnp.zeros((1, 128), F32)
        slots = []
        for b in range(NB):
            hit = jnp.max(
                jnp.where(listed == first_block + b, 1.0, 0.0).astype(F32), axis=0, keepdims=True
            )
            slots.append(jnp.where(hit > 0.5, run, 99.0))
            run = run + hit
        turned = jnp.concatenate(slots + [jnp.zeros((128 - NB, 128), F32)], axis=0).T
        for b in range(NB):
            slotb[b, rows, :] = jnp.broadcast_to(turned[:, b : b + 1], (128, 128))
        return carry

    lax.fori_loop(0, 4, prep, 0)

    sends = []
    count = [0]

    def rcopy(src, dst, dev):
        i = count[0]
        count[0] += 1
        copy = pltpu.make_async_remote_copy(
            src_ref=src,
            dst_ref=dst,
            send_sem=ssem.at[i],
            recv_sem=rsem.at[i],
            device_id=dev,
            device_id_type=MESH,
        )
        copy.start()
        sends.append(copy)
        return copy

    def reserve(k):
        i = count[0]
        count[0] += k
        return i

    def described(src, dst, dev, i):
        return pltpu.make_async_remote_copy(
            src_ref=src,
            dst_ref=dst,
            send_sem=ssem.at[i],
            recv_sem=rsem.at[i],
            device_id=dev,
            device_id_type=MESH,
        )

    loads[0].wait()
    pl.semaphore_wait(barrier, len(peers))

    act_at = reserve(8)

    def act_copy(d):
        return described(act.at[t], act.at[t], dev_t(d), act_at + d)

    for d in (4, 3, 5, 2, 6, 1, 7):
        sends.append(act_copy(d))
        sends[-1].start()
    loads[1].wait()

    def act_rows(yb):
        return jnp.concatenate([act[2 * yb], act[2 * yb + 1]], axis=0)

    def part16(n, k=16):
        return slice(n * k, (n + 1) * k)

    def rs_start(block, s, f, rp, rm):
        step_one, step_two = {}, {}
        far = (y + 2) % 4
        block(far, lambda n, cols, part: s.__setitem__(
            (pl.ds(n * 64 + far * 16, 16), slice(None), cols), part.astype(BF16)))
        for n in range(NC):
            step_one[n] = rcopy(
                s.at[pl.ds(n * 64 + far * 16, 16)],
                f.at[pl.ds(n * 16, 16)],
                dev_y(1 if n % 2 == 0 else 3),
            )
        for d in (1, 3):
            yb = (y + d) % 4

            def put(n, cols, part, d=d, yb=yb):
                if (n % 2 == 0) == (d == 1):
                    fo[part16(n), :, cols] = part
                else:
                    s[pl.ds(n * 64 + yb * 16, 16), :, cols] = part.astype(BF16)

            block(yb, put)

        def put_own(n, cols, part):
            own[part16(n), :, cols] = part

        def send(n, d):
            rows = pl.ds(n * 64 + ((y + d) % 4) * 16, 16)
            step_two[d, n] = rcopy(
                s.at[rows], (rp if d == 1 else rm).at[pl.ds(n * 16, 16)], dev_y(d)
            )

        for first in range(0, NC, 2):
            send(first, 3)
            send(first + 1, 1)
            if first == 0:
                block(y, put_own)
            for n, d in ((first, 1), (first + 1, 3)):
                rows = pl.ds(n * 64 + ((y + d) % 4) * 16, 16)
                step_one[n].wait_recv()
                s[rows] = (fo[part16(n)] + f[part16(n)].astype(F32)).astype(BF16)
                send(n, d)
        return step_two

    def rs_rest(y_in, rp, rm, sa, ra, ta, sb, rb, use):
        a_in, b_in = [], []
        for n in range(NC):
            for d in (1, 3):
                y_in[d, n].wait_recv()
            total = own[part16(n)] + rp[part16(n)].astype(F32) + rm[part16(n)].astype(F32)
            t1[part16(n)] = total
            sa[part16(n)] = total.astype(BF16)
            far = 2 if n % 2 == 0 else 14
            a_in.append(
                [
                    rcopy(
                        sa.at[pl.ds(n * 16 + ((k0 + dz) % 4) * 4, 4)],
                        ra.at[pl.ds((j * NC + n) * 4, 4)],
                        dev_z(dz),
                    )
                    for j, dz in ((2, far), (0, 1), (1, 15))
                ]
            )
        for n in range(NC):
            for copy in a_in[n]:
                copy.wait_recv()
            total = t1[pl.ds(n * 16 + k0 * 4, 4)]
            for j in range(3):
                total = total + ra[part16(j * NC + n, 4)].astype(F32)
            ta[part16(n, 4)] = total
            if sb is not ta:
                sb[part16(n, 4)] = total.astype(BF16)
            b_in.append(
                [
                    rcopy(
                        sb.at[pl.ds(n * 4 + (m0 + dm) % 4, 1)],
                        rb.at[pl.ds((dm - 1) * NC + n, 1)],
                        dev_z(4 * dm),
                    )
                    for dm in (2, 1, 3)
                ]
            )
        for n in range(NC):
            for copy in b_in[n]:
                copy.wait_recv()
            total = ta[n * 4 + m0]
            for dm in range(3):
                total = total + rb[dm * NC + n].astype(F32)
            use(n, total)

    def piece(dy, dz):
        zz = (z + dz) % NZ
        return pl.ds(((y + dy) % NY) * 16 + (zz % 4) * 4 + zz // 4, 1)

    class Gather:
        def __init__(self, g):
            self.g = g
            self.order = []
            self.y_in = []
            self.far_in = []
            self.z_in = {d: self.send(0, 0, dev_z(d)) for d in (8, 4, 12, 2, 14, 1, 15)}
            self.to_y(0)

        def send(self, dy, dz, dev):
            ref = self.g.at[piece(dy, dz)]
            return rcopy(ref, ref, dev)

        def to_y(self, dz):
            self.order.append(dz)
            self.y_in.append({d: self.send(0, dz, dev_y(d)) for d in (1, 3)})

        def arrived(self, copy, dz):
            copy.wait_recv()
            self.to_y(dz)

        def near(self):
            for d, dz in ((1, 15), (15, 1), (2, 14), (14, 2)):
                self.arrived(self.z_in[d], dz)

        def distant(self):
            self.z_in[4].wait_recv()
            low = [self.send(0, 12, dev_z(d)) for d in (1, 15, 2)]
            self.to_y(12)
            self.z_in[12].wait_recv()
            high = [self.send(0, 4, dev_z(d)) for d in (1, 15, 14)]
            self.to_y(4)
            self.forward(5)
            for copy, dz in ((low[0], 11), (high[0], 3), (low[1], 13), (high[1], 5)):
                self.arrived(copy, dz)
            self.z_in[8].wait_recv()
            across = [self.send(0, 8, dev_z(d)) for d in (1, 15)]
            self.to_y(8)
            self.arrived(low[2], 10)
            self.arrived(high[2], 6)
            self.forward(7)
            self.arrived(across[0], 7)
            self.arrived(across[1], 9)

        def forward(self, upto=16):
            for j in range(len(self.far_in), upto):
                d = 1 if j % 2 == 0 else 3
                self.y_in[j][d].wait_recv()
                self.far_in.append(self.send(4 - d, self.order[j], dev_y(d)))

        def wait(self, d):
            if d == 2:
                for copy in self.far_in:
                    copy.wait_recv()
            elif d > 0:
                for j in range(16):
                    if (j % 2 == 0) != (d == 1):
                        self.y_in[j][d].wait_recv()

        def block(self, d):
            yb = (y + 4 - d) % 4
            rows = self.g[pl.ds(yb * 16, 16)]
            return yb, rows.astype(F32).reshape(128, 1024).astype(BF16)

    def down_block(yb, put):
        for half in range(2):
            d = (t + 8 - (2 * yb + half)) % 8

            @pl.when(d != 0)
            def _(d=d):
                act_copy(d).wait_recv()

        for n in range(NC):
            part = jnp.dot(act_rows(yb), w[:, n * CW : (n + 1) * CW], preferred_element_type=F32)
            put(n, slice(None), part.reshape(16, 8, CW))

    y_in = rs_start(down_block, s1, f1, rp1, rm1)
    for i in range(8):
        actt[:, i * 64 : (i + 1) * 64] = act[i].astype(F32).T.astype(BF16)
    loads[2].wait()

    def use_hidden(n, total):
        hid[:, n * CW : (n + 1) * CW] = res[:, n * CW : (n + 1) * CW].astype(F32) + total

    rs_rest(y_in, rp1, rm1, s1a, ra1, t1a, t1a, rb1, use_hidden)

    mine = y * 16 + k0 * 4 + m0
    nrm[mine] = (hid[...] * gain_ref[...]).astype(BF16)
    nrm_all = Gather(nrm)
    h = hid[...]
    ssq[t] = jnp.broadcast_to(jnp.sum(h * h, axis=1, keepdims=True), (8, 128))
    ss_in = [rcopy(ssq.at[t], ssq.at[t], dev_t(d)) for d in (4, 3, 5, 2, 6, 1, 7)]
    nrm_all.near()
    for copy in ss_in:
        copy.wait_recv()
    square = ssq[0]
    for i in range(1, 8):
        square = square + ssq[i]
    inv_rms = lax.rsqrt(square / D + 1e-06)
    spot = lax.broadcasted_iota(jnp.int32, (8, 128), 1) == (
        lax.broadcasted_iota(jnp.int32, (8, 128), 0) + (k0 * 4 + m0) * 8
    )
    iv[z] = jnp.sum(jnp.where(spot, inv_rms, 0.0), axis=0, keepdims=True)
    inv_rms = inv_rms[:, :1]
    iv_in = [rcopy(iv.at[z], iv.at[z], dev_z(d)) for d in (8, 7, 9, 6, 10, 5, 11, 4, 12, 3, 13, 2, 14, 1, 15)]
    nrm_all.distant()
    for copy in iv_in:
        copy.wait_recv()
    inv_row = iv[0]
    for i in range(1, NZ):
        inv_row = inv_row + iv[i]
    ivy[y] = inv_row
    ivy_in = [rcopy(ivy.at[y], ivy.at[y], dev_y(d)) for d in (2, 1, 3)]
    loads[3].wait()

    order = (0, 1, 3, 2)
    lx_at = reserve(4)
    p_in = []
    def x_copy(dx):
        return described(lx.at[(x + dx) % 4], lxr.at[dx], dev_x(dx), lx_at + dx)

    def combine(copy, row_block):
        copy.wait_recv()
        lx[row_block] = lx[row_block] + lpr[row_block]
        dx = (row_block + 4 - x) % 4

        @pl.when(dx != 0)
        def _():
            x_copy(dx).start()

    blocks = []
    for d in order:
        nrm_all.wait(d)
        yb, block = nrm_all.block(d)
        lhs[...] = block

        def columns(j, carry):
            cols = pl.ds(pl.multiple_of(j * 256, 256), 256)
            lb[:, cols] = jnp.dot(lhs[...], head[:, cols], preferred_element_type=F32)
            return carry

        lax.fori_loop(0, 5, columns, 0)

        def compact(half, dst):
            rows = pl.ds(pl.multiple_of(half * 64, 64), 64)
            mask_rows = pl.ds(pl.multiple_of(yb * 128 + half * 64, 64), 64)
            out = [jnp.zeros((64, 128), F32) for _ in range(CAP)]
            for b in range(NB):
                slot = slotb[b, mask_rows, :]
                val = lb[rows, b * BLK : (b + 1) * BLK]
                for s in range(CAP):
                    out[s] = jnp.where(slot == float(s), val, out[s])
            for s in range(CAP):
                dst[:, s * BLK : (s + 1) * BLK] = out[s]

        compact(1 - c, lp.at[yb])
        p_in.append(rcopy(lp.at[yb], lpr.at[yb], partner))
        compact(c, lx.at[yb])
        blocks.append(yb)
        if d == 0:
            nrm_all.forward()
        if d != 1:
            while blocks:
                combine(p_in[-len(blocks)], blocks[0])
                blocks = blocks[1:]

    for copy in ivy_in:
        copy.wait_recv()
    scale_row = ivy[t // 2]
    turned = lax.broadcasted_iota(jnp.int32, (64, 128), 1) == (
        lax.broadcasted_iota(jnp.int32, (64, 128), 0) + c * 64
    )
    scale = jnp.sum(jnp.where(turned, scale_row, 0.0), axis=1, keepdims=True)
    total = lx[x]
    for dx in (1, 3, 2):
        x_copy(dx).wait_recv()
        total = total + lxr[dx]
    for dx in (1, 3, 2):
        x_copy(dx).wait_send()
    lg[...] = total * scale

    own_rows = pl.ds(pl.multiple_of(t * 64, 64), 64)
    lane = lax.broadcasted_iota(jnp.int32, (64, 128), 1)
    eye = lane == lax.broadcasted_iota(jnp.int32, (64, 128), 0)

    def to_row(col):
        return jnp.sum(jnp.where(eye, col, 0.0), axis=0, keepdims=True)

    def to_col(row):
        return jnp.sum(jnp.where(eye, row, 0.0), axis=1, keepdims=True)

    small_eye = lax.broadcasted_iota(jnp.int32, (64, 64), 0) == lax.broadcasted_iota(
        jnp.int32, (64, 64), 1
    )
    tok = jnp.sum(jnp.where(small_eye, tok_ref[...].astype(F32), 0.0), axis=1, keepdims=True)
    tok = tok.astype(jnp.int32)
    tok_block = (tok >> 7) - first_block
    tok_lane = tok & 127
    seen = jnp.zeros((64, 128), F32)
    tok_slot = jnp.full((64, 128), 99.0, F32)
    for b in range(NB):
        slot = slotb[b, own_rows, :]
        seen = seen + jnp.where(slot < 50.0, 1.0, 0.0)
        tok_slot = jnp.where(tok_block == b, slot, tok_slot)

    peak = jnp.full((64, 128), NEG, F32)
    for s in range(CAP):
        peak = jnp.maximum(peak, jnp.where(seen > float(s), lg[:, s * BLK : (s + 1) * BLK], NEG))
    peak = jnp.max(peak, axis=1, keepdims=True)
    zero = jnp.zeros((64, 128), F32)
    tot, mom, tgt = zero, zero, zero
    for s in range(CAP):
        val = lg[:, s * BLK : (s + 1) * BLK]
        ok = seen > float(s)
        shifted = jnp.where(ok, val - peak, 0.0)
        e = jnp.where(ok, jnp.exp(shifted), 0.0)
        tot = tot + e
        mom = mom + e * shifted
        tgt = tgt + jnp.where((tok_slot == float(s)) & (lane == tok_lane), val, 0.0)
    tot = jnp.sum(tot, axis=1, keepdims=True)
    mom = jnp.sum(mom, axis=1, keepdims=True)
    tgt = jnp.sum(tgt, axis=1, keepdims=True)
    stz[z] = jnp.concatenate([to_row(peak), to_row(tot), to_row(mom), to_row(tgt)], axis=0)
    st_in = [
        rcopy(stz.at[z], stz.at[z], dev_z(d))
        for d in (8, 7, 9, 6, 10, 5, 11, 4, 12, 3, 13, 2, 14, 1, 15)
    ]
    for copy in st_in:
        copy.wait_recv()

    def join(parts):
        top = parts[0][0:1]
        for p in parts[1:]:
            top = jnp.maximum(top, p[0:1])
        tot = jnp.zeros((1, 128), F32)
        mom = jnp.zeros((1, 128), F32)
        tgt = jnp.zeros((1, 128), F32)
        for p in parts:
            gap = p[0:1] - top
            scale = jnp.exp(gap)
            tot = tot + p[1:2] * scale
            mom = mom + scale * (p[2:3] + p[1:2] * gap)
            tgt = tgt + p[3:4]
        return top, tot, mom, tgt

    top, tot, mom, tgt = join([stz[i] for i in range(NZ)])
    sty[y] = jnp.concatenate([top, tot, mom, tgt], axis=0)
    y_st = [rcopy(sty.at[y], sty.at[y], dev_y(d)) for d in (2, 1, 3)]
    for copy in y_st:
        copy.wait_recv()
    top, tot, mom, tgt = join([sty[i] for i in range(NY)])
    top, tot, mom, tgt = to_col(top), to_col(tot), to_col(mom), to_col(tgt)

    response = t // 2
    length = jnp.int32(0)
    code = jnp.int32(0)
    length_sum = jnp.int32(0)
    for i in range(4):
        length = jnp.where(response == i, len_ref[i], length)
        code = jnp.where(response == i, adv_ref[i], code)
        length_sum = length_sum + len_ref[i]
    position = c * 64 + lax.broadcasted_iota(jnp.int32, (64, 1), 0)
    weight = jnp.where(position < length, code.astype(F32) / 32.0, 0.0)
    log_prob = tgt - top - jnp.log(tot)
    part = jnp.sum(weight * log_prob, axis=0, keepdims=True)
    gdot = weight * (mom / tot - (tgt - top))
    for s in range(CAP):
        val = lg[:, s * BLK : (s + 1) * BLK]
        prob = jnp.where(seen > float(s), jnp.exp(val - top), 0.0) / tot
        hot = jnp.where((tok_slot == float(s)) & (lane == tok_lane), 1.0, 0.0)
        dl[t, :, s * BLK : (s + 1) * BLK] = (weight * (prob - hot)).astype(BF16)
    dx_in = {d: rcopy(dl.at[t], dl.at[t], dev_x(d)) for d in (2, 1, 3)}
    d_in = {0: rcopy(dl.at[t], dl.at[t], partner)}
    gv[t] = to_row(gdot)
    g_in = [rcopy(gv.at[t], gv.at[t], dev_t(d)) for d in (4, 3, 5, 2, 6, 1, 7)]
    los[t] = jnp.broadcast_to(part, (8, 128))
    loss_in = [rcopy(los.at[t], los.at[t], dev_t(d)) for d in range(1, 8)]
    for d in (1, 3, 2):
        dx_in[d].wait_recv()
        slot = ((x + 4 - d) % 4) * 2 + c
        d_in[d] = rcopy(dl.at[slot], dl.at[slot], partner)
    for d in range(4):
        d_in[d].wait_recv()

    def head_block(yb, put):
        for half in range(2):
            rows = slice(half * 64, (half + 1) * 64)
            mask_rows = pl.ds(pl.multiple_of(yb * 128 + half * 64, 64), 64)
            vals = [
                dl[yb * 2 + half, :, s * BLK : (s + 1) * BLK].astype(F32) for s in range(CAP)
            ]
            for b in range(NB):
                slot = slotb[b, mask_rows, :]
                out = jnp.zeros((64, 128), F32)
                for s in range(CAP):
                    out = jnp.where(slot == float(s), vals[s], out)
                lhs2[rows, b * BLK : (b + 1) * BLK] = out.astype(BF16)
        for n in range(NC):
            for q in range(CW // 256):
                part = lax.dot_general(
                    lhs2[...],
                    head[n * CW + q * 256 : n * CW + (q + 1) * 256, :],
                    NT,
                    preferred_element_type=F32,
                )
                put(n, slice(q * 256, (q + 1) * 256), part.reshape(16, 8, 256))

    y_in = rs_start(head_block, s2, f2, rp2, rm2)
    for copy in g_in:
        copy.wait_recv()
    spot = lax.broadcasted_iota(jnp.int32, (8, 128), 1) == (
        lax.broadcasted_iota(jnp.int32, (8, 128), 0) + ((k0 % 2) * 4 + m0) * 8
    )
    gcol = jnp.sum(jnp.where(spot, gv[y * 2 + k0 // 2], 0.0), axis=1, keepdims=True)

    def use_dnormed(n, total):
        cols = slice(n * CW, (n + 1) * CW)
        value = inv_rms * (gain_ref[:, cols] * total) - hid[:, cols] * (
            inv_rms * inv_rms * gcol / D
        )
        dhg[mine, :, cols] = value.astype(BF16)

    rs_rest(y_in, rp2, rm2, s2a, ra2, t1b, s2b, rb2, use_dnormed)
    dhg_all = Gather(dhg)
    dhg_all.near()
    dhg_all.distant()

    ag_at = reserve(8)

    def ag_copy(d):
        return described(agr.at[(t + d) % 8], agr.at[8 + d], dev_t(d), ag_at + d)

    for d in order:
        dhg_all.wait(d)
        yb, block = dhg_all.block(d)
        dh[pl.ds(pl.multiple_of(yb * 128, 128), 128), :] = block
        part_a = lax.dot_general(block, w[...], NT, preferred_element_type=F32)
        ags[2 * yb] = part_a[:64]
        ags[2 * yb + 1] = part_a[64:]
        agr[2 * yb] = part_a[:64].astype(BF16)
        agr[2 * yb + 1] = part_a[64:].astype(BF16)
        for half in range(2):
            to = (2 * yb + half + 8 - t) % 8

            @pl.when(to != 0)
            def _(to=to):
                ag_copy(to).start()

        if d == order[0]:
            dhg_all.forward()
    dg_ref[...] = jnp.dot(actt[...], dh[...], preferred_element_type=F32).astype(BF16)
    for copy in loss_in:
        copy.wait_recv()
    objective = los[0]
    for i in range(1, 8):
        objective = objective + los[i]
    loss_ref[...] = -objective / length_sum.astype(F32)
    total = ags[t]
    for d in range(1, 8):
        ag_copy(d).wait_recv()
        total = total + agr[8 + d].astype(F32)
    ag_ref[...] = total.astype(BF16)
    for d in range(1, 8):
        ag_copy(d).wait_send()
    for copy in sends:
        copy.wait_send()


def last(dg, ag, loss, loss_ref, dg_ref, ag_ref):
    dg_ref[...] = dg[...]
    ag_ref[...] = ag[...]
    loss_ref[...] = loss[0:1, 0:1]


def body(
    residual,
    activation,
    down_weight,
    norm_gain,
    head_weight,
    allowed,
    tokens,
    lengths,
    advantage_code,
):
    any_spec = pl.BlockSpec(memory_space=pl.ANY)
    vmem = pl.BlockSpec(memory_space=pltpu.VMEM)
    smem = pl.BlockSpec(memory_space=pltpu.SMEM)
    v = pltpu.VMEM
    out = pl.pallas_call(
        kernel,
        out_shape=(
            jax.ShapeDtypeStruct((256, 1024), BF16),
            jax.ShapeDtypeStruct((64, 256), BF16),
            jax.ShapeDtypeStruct((8, 128), F32),
        ),
        in_specs=[any_spec, any_spec, any_spec, vmem, any_spec, vmem, vmem, smem, smem],
        out_specs=(vmem, vmem, vmem),
        scratch_shapes=[
            v((256, 512), BF16),
            v((512, 1024), BF16),
            v((8, 1024), BF16),
            v((8, 64, 256), BF16),
            v((256, 1024), BF16),
            v((1024, 1280), BF16),
            v((NB, 512, 128), F32),
            v((NC * 16, 8, CW), F32),
            v((NC * 16, 8, CW), F32),
            v((NC * 64, 8, CW), BF16),
            v((NC * 16, 8, CW), BF16),
            v((NC * 16, 8, CW), BF16),
            v((NC * 16, 8, CW), BF16),
            v((NC * 16, 8, CW), F32),
            v((NC * 16, 8, CW), BF16),
            v((3 * NC * 4, 8, CW), BF16),
            v((NC * 4, 8, CW), F32),
            v((NC * 4, 8, CW), F32),
            v((3 * NC, 8, CW), F32),
            v((8, 1024), F32),
            v((8, 8, 128), F32),
            v((NZ, 1, 128), F32),
            v((NY, 1, 128), F32),
            v((64, 8, 1024), BF16),
            v((NC * 64, 8, CW), BF16),
            v((NC * 16, 8, CW), BF16),
            v((NC * 16, 8, CW), BF16),
            v((NC * 16, 8, CW), BF16),
            v((NC * 16, 8, CW), BF16),
            v((3 * NC * 4, 8, CW), BF16),
            v((NC * 4, 8, CW), BF16),
            v((3 * NC, 8, CW), BF16),
            v((64, 8, 1024), BF16),
            v((128, 1024), BF16),
            v((128, 1280), F32),
            v((4, 64, CAP * BLK), F32),
            v((4, 64, CAP * BLK), F32),
            v((4, 64, CAP * BLK), F32),
            v((4, 64, CAP * BLK), F32),
            v((64, CAP * BLK), F32),
            v((NZ, 4, 128), F32),
            v((NY, 4, 128), F32),
            v((8, 64, CAP * BLK), BF16),
            v((8, 1, 128), F32),
            v((128, 1280), BF16),
            v((8, 64, 256), F32),
            v((16, 64, 256), BF16),
            v((8, 8, 128), F32),
            pltpu.SemaphoreType.DMA((4,)),
            pltpu.SemaphoreType.DMA((N_SEND,)),
            pltpu.SemaphoreType.DMA((N_SEND,)),
        ],
        compiler_params=pltpu.CompilerParams(
            collective_id=0, has_side_effects=True, vmem_limit_bytes=60 * 1024 * 1024
        ),
        name="step",
    )(
        residual.reshape(64, 8, 1024),
        activation,
        down_weight,
        norm_gain.reshape(1, 1024),
        head_weight,
        allowed.T,
        tokens.reshape(1, 64),
        lengths,
        advantage_code,
    )
    loss, dg, ag = pl.pallas_call(
        last,
        out_shape=(
            jax.ShapeDtypeStruct((1, 1), F32),
            jax.ShapeDtypeStruct((256, 1024), BF16),
            jax.ShapeDtypeStruct((64, 256), BF16),
        ),
        in_specs=[vmem] * 3,
        out_specs=(vmem, vmem, vmem),
        name="last",
    )(*out)
    return loss.reshape(()), dg, ag


def solution(mesh):
    in_specs = (
        P(None, "tp"),
        P("tp", "vocab"),
        P("vocab", "tp"),
        P("tp"),
        P("tp", "vocab"),
        P(),
        P("tp"),
        P(),
        P(),
    )
    out_specs = (P(), P("vocab", "tp"), P("tp", "vocab"))
    return jax.shard_map(body, mesh=mesh, in_specs=in_specs, out_specs=out_specs, check_vma=False)
```

```python
import jax
import jax.numpy as jnp
from jax import lax
from jax.experimental import pallas as pl
from jax.experimental.pallas import tpu as pltpu
from jax.sharding import PartitionSpec as P

MESH = pl.DeviceIdType.MESH
F32 = jnp.float32
BF16 = jnp.bfloat16
D = 8192
BLK = 128
CAP = 4
NB = 10
NY = 4
NZ = 16
NX = 4
NEG = -1e30
NC = 4
CW = 1024 // NC
N_SEND = 330
NT = (((1,), (1,)), ((), ()))


def kernel(
    res_hbm,
    act_hbm,
    w_hbm,
    gain_ref,
    head_hbm,
    allowed_ref,
    tok_ref,
    len_ref,
    adv_ref,
    dg_ref,
    ag_ref,
    loss_ref,
    actt,
    dh,
    res,
    act,
    w,
    head,
    slotb,
    own,
    fo,
    s1,
    f1,
    rp1,
    rm1,
    t1,
    s1a,
    ra1,
    t1a,
    t1b,
    rb1,
    hid,
    ssq,
    iv,
    ivy,
    nrm,
    s2,
    f2,
    rp2,
    rm2,
    s2a,
    ra2,
    s2b,
    rb2,
    dhg,
    lhs,
    lb,
    lp,
    lpr,
    lx,
    lxr,
    lg,
    stz,
    sty,
    dl,
    gv,
    lhs2,
    ags,
    agr,
    los,
    lsem,
    ssem,
    rsem,
):
    v = lax.axis_index("vocab")
    t = lax.axis_index("tp")
    y = v // NZ
    z = v % NZ
    x = t // 2
    c = t % 2
    k0 = z % 4
    m0 = z // 4

    def dev_y(d):
        return (((y + d) % NY) * NZ + z, t)

    def dev_z(d):
        return (y * NZ + (z + d) % NZ, t)

    def dev_t(d):
        return (v, (t + d) % 8)

    def dev_x(d):
        return (v, ((x + d) % NX) * 2 + c)

    partner = (v, x * 2 + (1 - c))

    barrier = pltpu.get_barrier_semaphore()
    peers = (
        [dev_t(d) for d in range(1, 8)]
        + [dev_y(d) for d in range(1, 4)]
        + [dev_z(d) for d in range(1, NZ)]
    )
    for dev in peers:
        pl.semaphore_signal(barrier, inc=1, device_id=dev, device_id_type=MESH)

    loads = [
        pltpu.make_async_copy(act_hbm, act.at[t], lsem.at[0]),
        pltpu.make_async_copy(w_hbm, w, lsem.at[1]),
        pltpu.make_async_copy(res_hbm.at[y * 16 + k0 * 4 + m0], res, lsem.at[2]),
        pltpu.make_async_copy(head_hbm, head, lsem.at[3]),
    ]
    for copy in loads:
        copy.start()

    first_block = v * NB

    def prep(i, carry):
        rows = pl.ds(pl.multiple_of(i * 128, 128), 128)
        listed = allowed_ref[:, rows]
        run = jnp.zeros((1, 128), F32)
        slots = []
        for b in range(NB):
            hit = jnp.max(
                jnp.where(listed == first_block + b, 1.0, 0.0).astype(F32), axis=0, keepdims=True
            )
            slots.append(jnp.where(hit > 0.5, run, 99.0))
            run = run + hit
        turned = jnp.concatenate(slots + [jnp.zeros((128 - NB, 128), F32)], axis=0).T
        for b in range(NB):
            slotb[b, rows, :] = jnp.broadcast_to(turned[:, b : b + 1], (128, 128))
        return carry

    lax.fori_loop(0, 4, prep, 0)

    sends = []
    count = [0]

    def rcopy(src, dst, dev):
        i = count[0]
        count[0] += 1
        copy = pltpu.make_async_remote_copy(
            src_ref=src,
            dst_ref=dst,
            send_sem=ssem.at[i],
            recv_sem=rsem.at[i],
            device_id=dev,
            device_id_type=MESH,
        )
        copy.start()
        sends.append(copy)
        return copy

    def reserve(k):
        i = count[0]
        count[0] += k
        return i

    def described(src, dst, dev, i):
        return pltpu.make_async_remote_copy(
            src_ref=src,
            dst_ref=dst,
            send_sem=ssem.at[i],
            recv_sem=rsem.at[i],
            device_id=dev,
            device_id_type=MESH,
        )

    loads[0].wait()
    pl.semaphore_wait(barrier, len(peers))

    act_at = reserve(8)

    def act_copy(d):
        return described(act.at[t], act.at[t], dev_t(d), act_at + d)

    for d in (4, 3, 5, 2, 6, 1, 7):
        sends.append(act_copy(d))
        sends[-1].start()
    loads[1].wait()

    def act_rows(yb):
        return jnp.concatenate([act[2 * yb], act[2 * yb + 1]], axis=0)

    def part16(n, k=16):
        return slice(n * k, (n + 1) * k)

    def rs_start(block, s, f, rp, rm):
        step_one, step_two = {}, {}
        far = (y + 2) % 4
        block(far, lambda n, cols, part: s.__setitem__(
            (pl.ds(n * 64 + far * 16, 16), slice(None), cols), part.astype(BF16)))
        for n in range(NC):
            step_one[n] = rcopy(
                s.at[pl.ds(n * 64 + far * 16, 16)],
                f.at[pl.ds(n * 16, 16)],
                dev_y(1 if n % 2 == 0 else 3),
            )
        for d in (1, 3):
            yb = (y + d) % 4

            def put(n, cols, part, d=d, yb=yb):
                if (n % 2 == 0) == (d == 1):
                    fo[part16(n), :, cols] = part
                else:
                    s[pl.ds(n * 64 + yb * 16, 16), :, cols] = part.astype(BF16)

            block(yb, put)

        def put_own(n, cols, part):
            own[part16(n), :, cols] = part

        def send(n, d):
            rows = pl.ds(n * 64 + ((y + d) % 4) * 16, 16)
            step_two[d, n] = rcopy(
                s.at[rows], (rp if d == 1 else rm).at[pl.ds(n * 16, 16)], dev_y(d)
            )

        for first in range(0, NC, 2):
            send(first, 3)
            send(first + 1, 1)
            if first == 0:
                block(y, put_own)
            for n, d in ((first, 1), (first + 1, 3)):
                rows = pl.ds(n * 64 + ((y + d) % 4) * 16, 16)
                step_one[n].wait_recv()
                s[rows] = (fo[part16(n)] + f[part16(n)].astype(F32)).astype(BF16)
                send(n, d)
        return step_two

    def rs_rest(y_in, rp, rm, sa, ra, ta, sb, rb, use):
        a_in, b_in = [], []
        for n in range(NC):
            for d in (1, 3):
                y_in[d, n].wait_recv()
            total = own[part16(n)] + rp[part16(n)].astype(F32) + rm[part16(n)].astype(F32)
            t1[part16(n)] = total
            sa[part16(n)] = total.astype(BF16)
            far = 2 if n % 2 == 0 else 14
            a_in.append(
                [
                    rcopy(
                        sa.at[pl.ds(n * 16 + ((k0 + dz) % 4) * 4, 4)],
                        ra.at[pl.ds((j * NC + n) * 4, 4)],
                        dev_z(dz),
                    )
                    for j, dz in ((2, far), (0, 1), (1, 15))
                ]
            )
        for n in range(NC):
            for copy in a_in[n]:
                copy.wait_recv()
            total = t1[pl.ds(n * 16 + k0 * 4, 4)]
            for j in range(3):
                total = total + ra[part16(j * NC + n, 4)].astype(F32)
            ta[part16(n, 4)] = total
            if sb is not ta:
                sb[part16(n, 4)] = total.astype(BF16)
            b_in.append(
                [
                    rcopy(
                        sb.at[pl.ds(n * 4 + (m0 + dm) % 4, 1)],
                        rb.at[pl.ds((dm - 1) * NC + n, 1)],
                        dev_z(4 * dm),
                    )
                    for dm in (2, 1, 3)
                ]
            )
        for n in range(NC):
            for copy in b_in[n]:
                copy.wait_recv()
            total = ta[n * 4 + m0]
            for dm in range(3):
                total = total + rb[dm * NC + n].astype(F32)
            use(n, total)

    def piece(dy, dz):
        zz = (z + dz) % NZ
        return pl.ds(((y + dy) % NY) * 16 + (zz % 4) * 4 + zz // 4, 1)

    class Gather:
        def __init__(self, g):
            self.g = g
            self.order = []
            self.y_in = []
            self.far_in = []
            self.z_in = {d: self.send(0, 0, dev_z(d)) for d in (8, 4, 12, 2, 14, 1, 15)}
            self.to_y(0)

        def send(self, dy, dz, dev):
            ref = self.g.at[piece(dy, dz)]
            return rcopy(ref, ref, dev)

        def to_y(self, dz):
            self.order.append(dz)
            self.y_in.append({d: self.send(0, dz, dev_y(d)) for d in (1, 3)})

        def arrived(self, copy, dz):
            copy.wait_recv()
            self.to_y(dz)

        def near(self):
            for d, dz in ((1, 15), (15, 1), (2, 14), (14, 2)):
                self.arrived(self.z_in[d], dz)

        def distant(self):
            self.z_in[4].wait_recv()
            low = [self.send(0, 12, dev_z(d)) for d in (1, 15, 2)]
            self.to_y(12)
            self.z_in[12].wait_recv()
            high = [self.send(0, 4, dev_z(d)) for d in (1, 15, 14)]
            self.to_y(4)
            self.forward(5)
            for copy, dz in ((low[0], 11), (high[0], 3), (low[1], 13), (high[1], 5)):
                self.arrived(copy, dz)
            self.z_in[8].wait_recv()
            across = [self.send(0, 8, dev_z(d)) for d in (1, 15)]
            self.to_y(8)
            self.arrived(low[2], 10)
            self.arrived(high[2], 6)
            self.forward(7)
            self.arrived(across[0], 7)
            self.arrived(across[1], 9)

        def forward(self, upto=16):
            for j in range(len(self.far_in), upto):
                d = 1 if j % 2 == 0 else 3
                self.y_in[j][d].wait_recv()
                self.far_in.append(self.send(4 - d, self.order[j], dev_y(d)))

        def wait(self, d):
            if d == 2:
                for copy in self.far_in:
                    copy.wait_recv()
            elif d > 0:
                for j in range(16):
                    if (j % 2 == 0) != (d == 1):
                        self.y_in[j][d].wait_recv()

        def block(self, d):
            yb = (y + 4 - d) % 4
            rows = self.g[pl.ds(yb * 16, 16)]
            return yb, rows.astype(F32).reshape(128, 1024).astype(BF16)

    def down_block(yb, put):
        for half in range(2):
            d = (t + 8 - (2 * yb + half)) % 8

            @pl.when(d != 0)
            def _(d=d):
                act_copy(d).wait_recv()

        for n in range(NC):
            part = jnp.dot(act_rows(yb), w[:, n * CW : (n + 1) * CW], preferred_element_type=F32)
            put(n, slice(None), part.reshape(16, 8, CW))

    y_in = rs_start(down_block, s1, f1, rp1, rm1)
    for i in range(8):
        actt[:, i * 64 : (i + 1) * 64] = act[i].astype(F32).T.astype(BF16)
    loads[2].wait()

    def use_hidden(n, total):
        hid[:, n * CW : (n + 1) * CW] = res[:, n * CW : (n + 1) * CW].astype(F32) + total

    rs_rest(y_in, rp1, rm1, s1a, ra1, t1a, t1a, rb1, use_hidden)

    mine = y * 16 + k0 * 4 + m0
    nrm[mine] = (hid[...] * gain_ref[...]).astype(BF16)
    nrm_all = Gather(nrm)
    h = hid[...]
    ssq[t] = jnp.broadcast_to(jnp.sum(h * h, axis=1, keepdims=True), (8, 128))
    ss_in = [rcopy(ssq.at[t], ssq.at[t], dev_t(d)) for d in (4, 3, 5, 2, 6, 1, 7)]
    nrm_all.near()
    for copy in ss_in:
        copy.wait_recv()
    square = ssq[0]
    for i in range(1, 8):
        square = square + ssq[i]
    inv_rms = lax.rsqrt(square / D + 1e-06)
    spot = lax.broadcasted_iota(jnp.int32, (8, 128), 1) == (
        lax.broadcasted_iota(jnp.int32, (8, 128), 0) + (k0 * 4 + m0) * 8
    )
    iv[z] = jnp.sum(jnp.where(spot, inv_rms, 0.0), axis=0, keepdims=True)
    inv_rms = inv_rms[:, :1]
    iv_in = [rcopy(iv.at[z], iv.at[z], dev_z(d)) for d in (8, 7, 9, 6, 10, 5, 11, 4, 12, 3, 13, 2, 14, 1, 15)]
    nrm_all.distant()
    for copy in iv_in:
        copy.wait_recv()
    inv_row = iv[0]
    for i in range(1, NZ):
        inv_row = inv_row + iv[i]
    ivy[y] = inv_row
    ivy_in = [rcopy(ivy.at[y], ivy.at[y], dev_y(d)) for d in (2, 1, 3)]
    loads[3].wait()

    order = (0, 1, 3, 2)
    lx_at = reserve(4)
    p_in = []
    def x_copy(dx):
        return described(lx.at[(x + dx) % 4], lxr.at[dx], dev_x(dx), lx_at + dx)

    def combine(copy, row_block):
        copy.wait_recv()
        lx[row_block] = lx[row_block] + lpr[row_block]
        dx = (row_block + 4 - x) % 4

        @pl.when(dx != 0)
        def _():
            x_copy(dx).start()

    blocks = []
    for d in order:
        nrm_all.wait(d)
        yb, block = nrm_all.block(d)
        lhs[...] = block

        def columns(j, carry):
            cols = pl.ds(pl.multiple_of(j * 256, 256), 256)
            lb[:, cols] = jnp.dot(lhs[...], head[:, cols], preferred_element_type=F32)
            return carry

        lax.fori_loop(0, 5, columns, 0)

        def compact(half, dst):
            rows = pl.ds(pl.multiple_of(half * 64, 64), 64)
            mask_rows = pl.ds(pl.multiple_of(yb * 128 + half * 64, 64), 64)
            out = [jnp.zeros((64, 128), F32) for _ in range(CAP)]
            for b in range(NB):
                slot = slotb[b, mask_rows, :]
                val = lb[rows, b * BLK : (b + 1) * BLK]
                for s in range(CAP):
                    out[s] = jnp.where(slot == float(s), val, out[s])
            for s in range(CAP):
                dst[:, s * BLK : (s + 1) * BLK] = out[s]

        compact(1 - c, lp.at[yb])
        p_in.append(rcopy(lp.at[yb], lpr.at[yb], partner))
        compact(c, lx.at[yb])
        blocks.append(yb)
        if d == 0:
            nrm_all.forward()
        if d != 1:
            while blocks:
                combine(p_in[-len(blocks)], blocks[0])
                blocks = blocks[1:]

    for copy in ivy_in:
        copy.wait_recv()
    scale_row = ivy[t // 2]
    turned = lax.broadcasted_iota(jnp.int32, (64, 128), 1) == (
        lax.broadcasted_iota(jnp.int32, (64, 128), 0) + c * 64
    )
    scale = jnp.sum(jnp.where(turned, scale_row, 0.0), axis=1, keepdims=True)
    total = lx[x]
    for dx in (1, 3, 2):
        x_copy(dx).wait_recv()
        total = total + lxr[dx]
    for dx in (1, 3, 2):
        x_copy(dx).wait_send()
    lg[...] = total * scale

    own_rows = pl.ds(pl.multiple_of(t * 64, 64), 64)
    lane = lax.broadcasted_iota(jnp.int32, (64, 128), 1)
    eye = lane == lax.broadcasted_iota(jnp.int32, (64, 128), 0)

    def to_row(col):
        return jnp.sum(jnp.where(eye, col, 0.0), axis=0, keepdims=True)

    def to_col(row):
        return jnp.sum(jnp.where(eye, row, 0.0), axis=1, keepdims=True)

    small_eye = lax.broadcasted_iota(jnp.int32, (64, 64), 0) == lax.broadcasted_iota(
        jnp.int32, (64, 64), 1
    )
    tok = jnp.sum(jnp.where(small_eye, tok_ref[...].astype(F32), 0.0), axis=1, keepdims=True)
    tok = tok.astype(jnp.int32)
    tok_block = (tok >> 7) - first_block
    tok_lane = tok & 127
    seen = jnp.zeros((64, 128), F32)
    tok_slot = jnp.full((64, 128), 99.0, F32)
    for b in range(NB):
        slot = slotb[b, own_rows, :]
        seen = seen + jnp.where(slot < 50.0, 1.0, 0.0)
        tok_slot = jnp.where(tok_block == b, slot, tok_slot)

    peak = jnp.full((64, 128), NEG, F32)
    for s in range(CAP):
        peak = jnp.maximum(peak, jnp.where(seen > float(s), lg[:, s * BLK : (s + 1) * BLK], NEG))
    peak = jnp.max(peak, axis=1, keepdims=True)
    zero = jnp.zeros((64, 128), F32)
    tot, mom, tgt = zero, zero, zero
    for s in range(CAP):
        val = lg[:, s * BLK : (s + 1) * BLK]
        ok = seen > float(s)
        shifted = jnp.where(ok, val - peak, 0.0)
        e = jnp.where(ok, jnp.exp(shifted), 0.0)
        tot = tot + e
        mom = mom + e * shifted
        tgt = tgt + jnp.where((tok_slot == float(s)) & (lane == tok_lane), val, 0.0)
    tot = jnp.sum(tot, axis=1, keepdims=True)
    mom = jnp.sum(mom, axis=1, keepdims=True)
    tgt = jnp.sum(tgt, axis=1, keepdims=True)
    stz[z] = jnp.concatenate([to_row(peak), to_row(tot), to_row(mom), to_row(tgt)], axis=0)
    st_in = [
        rcopy(stz.at[z], stz.at[z], dev_z(d))
        for d in (8, 7, 9, 6, 10, 5, 11, 4, 12, 3, 13, 2, 14, 1, 15)
    ]
    for copy in st_in:
        copy.wait_recv()

    def join(parts):
        top = parts[0][0:1]
        for p in parts[1:]:
            top = jnp.maximum(top, p[0:1])
        tot = jnp.zeros((1, 128), F32)
        mom = jnp.zeros((1, 128), F32)
        tgt = jnp.zeros((1, 128), F32)
        for p in parts:
            gap = p[0:1] - top
            scale = jnp.exp(gap)
            tot = tot + p[1:2] * scale
            mom = mom + scale * (p[2:3] + p[1:2] * gap)
            tgt = tgt + p[3:4]
        return top, tot, mom, tgt

    top, tot, mom, tgt = join([stz[i] for i in range(NZ)])
    sty[y] = jnp.concatenate([top, tot, mom, tgt], axis=0)
    y_st = [rcopy(sty.at[y], sty.at[y], dev_y(d)) for d in (2, 1, 3)]
    for copy in y_st:
        copy.wait_recv()
    top, tot, mom, tgt = join([sty[i] for i in range(NY)])
    top, tot, mom, tgt = to_col(top), to_col(tot), to_col(mom), to_col(tgt)

    response = t // 2
    length = jnp.int32(0)
    code = jnp.int32(0)
    length_sum = jnp.int32(0)
    for i in range(4):
        length = jnp.where(response == i, len_ref[i], length)
        code = jnp.where(response == i, adv_ref[i], code)
        length_sum = length_sum + len_ref[i]
    position = c * 64 + lax.broadcasted_iota(jnp.int32, (64, 1), 0)
    weight = jnp.where(position < length, code.astype(F32) / 32.0, 0.0)
    log_prob = tgt - top - jnp.log(tot)
    part = jnp.sum(weight * log_prob, axis=0, keepdims=True)
    gdot = weight * (mom / tot - (tgt - top))
    for s in range(CAP):
        val = lg[:, s * BLK : (s + 1) * BLK]
        prob = jnp.where(seen > float(s), jnp.exp(val - top), 0.0) / tot
        hot = jnp.where((tok_slot == float(s)) & (lane == tok_lane), 1.0, 0.0)
        dl[t, :, s * BLK : (s + 1) * BLK] = (weight * (prob - hot)).astype(BF16)
    dx_in = {d: rcopy(dl.at[t], dl.at[t], dev_x(d)) for d in (2, 1, 3)}
    dl_at = reserve(4)

    def to_partner(slot, d):
        return described(dl.at[slot], dl.at[slot], partner, dl_at + d)

    sends.append(to_partner(t, 0))
    sends[-1].start()
    gv[t] = to_row(gdot)
    g_in = [rcopy(gv.at[t], gv.at[t], dev_t(d)) for d in (4, 3, 5, 2, 6, 1, 7)]
    los[t] = jnp.broadcast_to(part, (8, 128))
    loss_in = [rcopy(los.at[t], los.at[t], dev_t(d)) for d in range(1, 8)]
    for d in (1, 3, 2):
        dx_in[d].wait_recv()
        slot = ((x + 4 - d) % 4) * 2 + c
        sends.append(to_partner(slot, d))
        sends[-1].start()

    def head_block(yb, put):
        to_partner(t, (x + 4 - yb) % 4).wait_recv()
        for half in range(2):
            rows = slice(half * 64, (half + 1) * 64)
            mask_rows = pl.ds(pl.multiple_of(yb * 128 + half * 64, 64), 64)
            vals = [
                dl[yb * 2 + half, :, s * BLK : (s + 1) * BLK].astype(F32) for s in range(CAP)
            ]
            for b in range(NB):
                slot = slotb[b, mask_rows, :]
                out = jnp.zeros((64, 128), F32)
                for s in range(CAP):
                    out = jnp.where(slot == float(s), vals[s], out)
                lhs2[rows, b * BLK : (b + 1) * BLK] = out.astype(BF16)
        for n in range(NC):
            for q in range(CW // 256):
                part = lax.dot_general(
                    lhs2[...],
                    head[n * CW + q * 256 : n * CW + (q + 1) * 256, :],
                    NT,
                    preferred_element_type=F32,
                )
                put(n, slice(q * 256, (q + 1) * 256), part.reshape(16, 8, 256))

    y_in = rs_start(head_block, s2, f2, rp2, rm2)
    for copy in g_in:
        copy.wait_recv()
    spot = lax.broadcasted_iota(jnp.int32, (8, 128), 1) == (
        lax.broadcasted_iota(jnp.int32, (8, 128), 0) + ((k0 % 2) * 4 + m0) * 8
    )
    gcol = jnp.sum(jnp.where(spot, gv[y * 2 + k0 // 2], 0.0), axis=1, keepdims=True)

    def use_dnormed(n, total):
        cols = slice(n * CW, (n + 1) * CW)
        value = inv_rms * (gain_ref[:, cols] * total) - hid[:, cols] * (
            inv_rms * inv_rms * gcol / D
        )
        dhg[mine, :, cols] = value.astype(BF16)

    rs_rest(y_in, rp2, rm2, s2a, ra2, t1b, s2b, rb2, use_dnormed)
    dhg_all = Gather(dhg)
    dhg_all.near()
    dhg_all.distant()

    ag_at = reserve(8)

    def ag_copy(d):
        return described(agr.at[(t + d) % 8], agr.at[8 + d], dev_t(d), ag_at + d)

    for d in order:
        dhg_all.wait(d)
        yb, block = dhg_all.block(d)
        dh[pl.ds(pl.multiple_of(yb * 128, 128), 128), :] = block
        part_a = lax.dot_general(block, w[...], NT, preferred_element_type=F32)
        ags[2 * yb] = part_a[:64]
        ags[2 * yb + 1] = part_a[64:]
        agr[2 * yb] = part_a[:64].astype(BF16)
        agr[2 * yb + 1] = part_a[64:].astype(BF16)
        for half in range(2):
            to = (2 * yb + half + 8 - t) % 8

            @pl.when(to != 0)
            def _(to=to):
                ag_copy(to).start()

        if d == order[0]:
            dhg_all.forward()
    dg_ref[...] = jnp.dot(actt[...], dh[...], preferred_element_type=F32).astype(BF16)
    for copy in loss_in:
        copy.wait_recv()
    objective = los[0]
    for i in range(1, 8):
        objective = objective + los[i]
    loss_ref[...] = -objective / length_sum.astype(F32)
    total = ags[t]
    for d in range(1, 8):
        ag_copy(d).wait_recv()
        total = total + agr[8 + d].astype(F32)
    ag_ref[...] = total.astype(BF16)
    for d in range(1, 8):
        ag_copy(d).wait_send()
    for copy in sends:
        copy.wait_send()


def last(dg, ag, loss, loss_ref, dg_ref, ag_ref):
    dg_ref[...] = dg[...]
    ag_ref[...] = ag[...]
    loss_ref[...] = loss[0:1, 0:1]


def body(
    residual,
    activation,
    down_weight,
    norm_gain,
    head_weight,
    allowed,
    tokens,
    lengths,
    advantage_code,
):
    any_spec = pl.BlockSpec(memory_space=pl.ANY)
    vmem = pl.BlockSpec(memory_space=pltpu.VMEM)
    smem = pl.BlockSpec(memory_space=pltpu.SMEM)
    v = pltpu.VMEM
    out = pl.pallas_call(
        kernel,
        out_shape=(
            jax.ShapeDtypeStruct((256, 1024), BF16),
            jax.ShapeDtypeStruct((64, 256), BF16),
            jax.ShapeDtypeStruct((8, 128), F32),
        ),
        in_specs=[any_spec, any_spec, any_spec, vmem, any_spec, vmem, vmem, smem, smem],
        out_specs=(vmem, vmem, vmem),
        scratch_shapes=[
            v((256, 512), BF16),
            v((512, 1024), BF16),
            v((8, 1024), BF16),
            v((8, 64, 256), BF16),
            v((256, 1024), BF16),
            v((1024, 1280), BF16),
            v((NB, 512, 128), F32),
            v((NC * 16, 8, CW), F32),
            v((NC * 16, 8, CW), F32),
            v((NC * 64, 8, CW), BF16),
            v((NC * 16, 8, CW), BF16),
            v((NC * 16, 8, CW), BF16),
            v((NC * 16, 8, CW), BF16),
            v((NC * 16, 8, CW), F32),
            v((NC * 16, 8, CW), BF16),
            v((3 * NC * 4, 8, CW), BF16),
            v((NC * 4, 8, CW), F32),
            v((NC * 4, 8, CW), F32),
            v((3 * NC, 8, CW), F32),
            v((8, 1024), F32),
            v((8, 8, 128), F32),
            v((NZ, 1, 128), F32),
            v((NY, 1, 128), F32),
            v((64, 8, 1024), BF16),
            v((NC * 64, 8, CW), BF16),
            v((NC * 16, 8, CW), BF16),
            v((NC * 16, 8, CW), BF16),
            v((NC * 16, 8, CW), BF16),
            v((NC * 16, 8, CW), BF16),
            v((3 * NC * 4, 8, CW), BF16),
            v((NC * 4, 8, CW), BF16),
            v((3 * NC, 8, CW), BF16),
            v((64, 8, 1024), BF16),
            v((128, 1024), BF16),
            v((128, 1280), F32),
            v((4, 64, CAP * BLK), F32),
            v((4, 64, CAP * BLK), F32),
            v((4, 64, CAP * BLK), F32),
            v((4, 64, CAP * BLK), F32),
            v((64, CAP * BLK), F32),
            v((NZ, 4, 128), F32),
            v((NY, 4, 128), F32),
            v((8, 64, CAP * BLK), BF16),
            v((8, 1, 128), F32),
            v((128, 1280), BF16),
            v((8, 64, 256), F32),
            v((16, 64, 256), BF16),
            v((8, 8, 128), F32),
            pltpu.SemaphoreType.DMA((4,)),
            pltpu.SemaphoreType.DMA((N_SEND,)),
            pltpu.SemaphoreType.DMA((N_SEND,)),
        ],
        compiler_params=pltpu.CompilerParams(
            collective_id=0, has_side_effects=True, vmem_limit_bytes=60 * 1024 * 1024
        ),
        name="step",
    )(
        residual.reshape(64, 8, 1024),
        activation,
        down_weight,
        norm_gain.reshape(1, 1024),
        head_weight,
        allowed.T,
        tokens.reshape(1, 64),
        lengths,
        advantage_code,
    )
    loss, dg, ag = pl.pallas_call(
        last,
        out_shape=(
            jax.ShapeDtypeStruct((1, 1), F32),
            jax.ShapeDtypeStruct((256, 1024), BF16),
            jax.ShapeDtypeStruct((64, 256), BF16),
        ),
        in_specs=[vmem] * 3,
        out_specs=(vmem, vmem, vmem),
        name="last",
    )(*out)
    return loss.reshape(()), dg, ag


def solution(mesh):
    in_specs = (
        P(None, "tp"),
        P("tp", "vocab"),
        P("vocab", "tp"),
        P("tp"),
        P("tp", "vocab"),
        P(),
        P("tp"),
        P(),
        P(),
    )
    out_specs = (P(), P("vocab", "tp"), P("tp", "vocab"))
    return jax.shard_map(body, mesh=mesh, in_specs=in_specs, out_specs=out_specs, check_vma=False)
```
